32 devices in a mesh: chan: 8 (over z, core), tm: 4 (over y, x).
Axes of the slice: x: 2, y: 2, z: 4, core: 2. Of those that a mesh axis runs over, the one named last changes fastest.
Arguments:
- spectra: float32 [32, 16, 2048], P('chan', 'tm'), as said below
- keep_mask: int32 [32, 16], P('chan', 'tm'), may hold values from 0 to 1, as said below
Outputs:
- stacked: float32 [32, 32, 201], P('chan', 'tm')
The draws below stay inside these ranges and needn't reach their ends.
Inputs may be any that keep to these rules, and one draw needn't show every extreme that they name: `spectra`: real parts of the 1024 bins, then their imaginary parts, of each channel's and sub-window's spectrum. `keep_mask`: one or two channels are rejected in every sub-window; elsewhere the share of kept sub-windows rises along the time axis.
All inputs are finite; a program needn't handle non-finite values.
Results may differ from the reference program's by a relative error of at most 0.00066.
Values may be sent and summed in bfloat16 or wider, within the bound.
No kernel may reach another device: no remote copies, remote signals or barrier semaphores. Data moves between devices by JAX's collectives and lax.ppermute only.
A program may use at most 64 MiB of HBM per device.

```python
import math
import jax
import jax.numpy as jnp
from jax import lax

F = 1024
MAXLAG = 100
CHANNELS = 32
SUBWIN = 16


def draw_spectra(key, part):
    delay = jax.random.randint(jax.random.fold_in(key, 11), (CHANNELS, 1, 1), -(MAXLAG // 2), MAXLAG // 2 + 1)
    freq = jnp.arange(F, dtype=jnp.int32)[None, None, :] + 1
    phase = (freq * delay % (2 * F)).astype(jnp.float32) * (math.pi / F)
    source = jax.random.normal(jax.random.fold_in(key, 12), (2, 1, SUBWIN, F), jnp.float32)
    noise = jax.random.normal(jax.random.fold_in(key, 13), (2, CHANNELS, SUBWIN, F), jnp.float32)
    spread = math.log(10.0)
    amplitude = jnp.exp(jax.random.uniform(jax.random.fold_in(key, 14), (CHANNELS, SUBWIN, 1), jnp.float32, 0.0, spread))
    colour = jnp.exp(jax.random.uniform(jax.random.fold_in(key, 15), (CHANNELS, 1, F), jnp.float32, 0.0, math.log(4.0)))
    cosine = jnp.cos(phase)
    sine = jnp.sin(phase)
    real_part = 0.8 * (source[0] * cosine + source[1] * sine) + noise[0]
    imag_part = 0.8 * (source[1] * cosine - source[0] * sine) + noise[1]
    scale = amplitude * colour
    return jnp.concatenate([real_part * scale, imag_part * scale], axis=-1)


def draw_keep_mask(key, part):
    channel = jnp.arange(CHANNELS, dtype=jnp.int32)[:, None]
    window = jnp.arange(SUBWIN, dtype=jnp.int32)[None, :]
    level = 300 + 650 * window // max(SUBWIN - 1, 1)
    draws = jax.random.randint(jax.random.fold_in(key, 21), (CHANNELS, SUBWIN), 0, 1000)
    rejected = jax.random.randint(jax.random.fold_in(key, 22), (2,), 0, CHANNELS)
    alive = (channel != rejected[0]) & (channel != rejected[1])
    return ((draws < level) & alive).astype(jnp.int32)


def setup_inputs(seed: int = 0) -> dict:
    splits = jax.random.split(jax.random.key(seed), 3)
    spectra = draw_spectra(jax.random.fold_in(splits[2], 71), 0)
    keep_mask = draw_keep_mask(jax.random.fold_in(splits[2], 71), 0)
    return dict(spectra=spectra, keep_mask=keep_mask)


def lag_table(nbins, maxlag):
    freq = jnp.arange(nbins, dtype=jnp.int32) + 1
    shift = jnp.arange(2 * maxlag + 1, dtype=jnp.int32) - maxlag
    turns = freq[:, None] * shift[None, :] % (2 * nbins)
    theta = turns.astype(jnp.float32) * (jnp.pi / nbins)
    return jnp.concatenate([jnp.cos(theta), -jnp.sin(theta)], axis=0) / nbins

def whiten(spectra):
    nbins = spectra.shape[-1] // 2
    real_part = spectra[..., :nbins]
    imag_part = spectra[..., nbins:]
    power = real_part * real_part + imag_part * imag_part
    level = lax.optimization_barrier(jnp.mean(power, axis=-1, keepdims=True)) + 1e-06
    factor = lax.rsqrt(power + 0.5 * level)
    return spectra * jnp.concatenate([factor, factor], axis=-1)

def reference(spectra, keep_mask):
    table = lag_table(F, MAXLAG)
    maskf = keep_mask.astype(jnp.float32)
    white = (whiten(spectra) * maskf[:, :, None]).astype(jnp.bfloat16)
    wide = white.astype(jnp.float32)
    real_all = wide[..., :F]
    imag_all = wide[..., F:]
    high = lax.Precision.HIGHEST

    def one_row(index):
        real_one = lax.dynamic_index_in_dim(real_all, index, 0, keepdims=False)
        imag_one = lax.dynamic_index_in_dim(imag_all, index, 0, keepdims=False)
        cross_re = jnp.einsum('sf,jsf->jf', real_one, real_all, precision=high) + jnp.einsum('sf,jsf->jf', imag_one, imag_all, precision=high)
        cross_im = jnp.einsum('sf,jsf->jf', imag_one, real_all, precision=high) - jnp.einsum('sf,jsf->jf', real_one, imag_all, precision=high)
        lagged = jnp.dot(jnp.concatenate([cross_re, cross_im], axis=1), table, precision=high)
        mask_one = lax.dynamic_index_in_dim(maskf, index, 0, keepdims=False)
        pairs = jnp.dot(maskf, mask_one, precision=high)
        return lagged / jnp.maximum(pairs, 1.0)[:, None]
    return lax.map(one_row, jnp.arange(CHANNELS, dtype=jnp.int32))
```

```python
import jax
import jax.numpy as jnp
import ml_dtypes
import numpy as np
from jax import lax
from jax.experimental import pallas as pl
from jax.experimental.pallas import tpu as pltpu
from jax.sharding import PartitionSpec as P

MAXLAG = 100
LANES = 128
CORES = 2
NUM_LAGS = 2 * MAXLAG + 1
PADDED_LAGS = 256


def lag_tables(nbins):
    freq = np.arange(nbins, dtype=np.int64) + 1
    shift = np.arange(NUM_LAGS, dtype=np.int64) - MAXLAG
    theta = (freq[:, None] * shift[None, :] % (2 * nbins)) * (np.pi / nbins)
    cosine = (np.cos(theta) / nbins).reshape(nbins // LANES, LANES, NUM_LAGS)
    sine = (-np.sin(theta) / nbins).reshape(nbins // LANES, LANES, NUM_LAGS)
    table = np.concatenate([cosine, sine], axis=1).astype(np.float32)
    table = np.pad(table, ((0, 0), (0, 0), (0, PADDED_LAGS - NUM_LAGS)))
    high = table.astype(ml_dtypes.bfloat16)
    low = (table - high.astype(np.float32)).astype(ml_dtypes.bfloat16)
    return high, low


def whiten_kernel(mask_ref, spectra_ref, out_ref):
    channels, windows, width = spectra_ref.shape
    nbins = width // 2
    blocks = width // LANES
    row = lax.broadcasted_iota(jnp.int32, (windows, 1), 0)
    pieces = []
    masks = []
    for ch in range(channels):
        keep = jnp.zeros((windows, 1), jnp.float32)
        for s in range(windows):
            keep = jnp.where(row == s, mask_ref[ch, s].astype(jnp.float32), keep)
        spec = spectra_ref[ch]
        re = spec[:, :nbins]
        im = spec[:, nbins:]
        power = re * re + im * im
        level = jnp.mean(power, axis=-1, keepdims=True) + 1e-06
        factor = lax.rsqrt(power + 0.5 * level)
        pieces.append((re * factor * keep, im * factor * keep))
        masks.append(jnp.broadcast_to(keep, (windows, LANES)))
    re = jnp.concatenate([p[0] for p in pieces], axis=0).astype(jnp.bfloat16)
    im = jnp.concatenate([p[1] for p in pieces], axis=0).astype(jnp.bfloat16)
    half = blocks // 2
    for fb in range(half):
        out_ref[fb] = re[:, fb * LANES : (fb + 1) * LANES]
        out_ref[half + fb] = im[:, fb * LANES : (fb + 1) * LANES]
    out_ref[blocks] = jnp.concatenate(masks, axis=0).astype(jnp.bfloat16)


def whiten(spectra, keep_mask):
    channels, windows, width = spectra.shape
    return pl.pallas_call(
        whiten_kernel,
        out_shape=jax.ShapeDtypeStruct((width // LANES + 1, channels * windows, LANES), jnp.bfloat16),
        in_specs=[pl.BlockSpec(memory_space=pltpu.SMEM), pl.BlockSpec(memory_space=pltpu.VMEM)],
        out_specs=pl.BlockSpec(memory_space=pltpu.VMEM),
        name="whiten",
    )(keep_mask, spectra)


def correlate_kernel(groups, channels, windows, *refs):
    place_ref = refs[0]
    near_refs = refs[1 : 1 + groups]
    far_refs = refs[1 + groups : 3 + groups]
    high_ref, low_ref, out_ref, pattern_ref, lag_ref, pair_ref = refs[3 + groups :]
    blocks = near_refs[0].shape[0] - 1
    half = blocks // 2
    duos = channels // 2
    rows = 2 * windows
    upper = lax.broadcasted_iota(jnp.int32, (rows, LANES), 0) < windows

    for k in range(groups):
        for fb in range(blocks + 1):
            wide = near_refs[k][fb].astype(jnp.float32)
            for duo in range(duos):
                tile = wide[duo * rows : (duo + 1) * rows]
                turned = pltpu.roll(tile, windows, 0)
                pattern_ref[k, fb, 2 * duo] = jnp.where(upper, tile, turned)
                pattern_ref[k, fb, 2 * duo + 1] = jnp.where(upper, turned, tile)

    swap = place_ref[0]
    total = jnp.zeros((channels * 2 * duos * rows, PADDED_LAGS), jnp.float32)
    for fb in range(half):
        lines = {}
        for side in range(2):
            acc = {}
            for b in range(groups):
                k = lax.bitwise_xor(swap, b)
                far_re = far_refs[side][b, fb].astype(jnp.float32)
                far_im = far_refs[side][b, half + fb].astype(jnp.float32)
                for i in range(channels):
                    near_re = pattern_ref[k, fb, i]
                    near_im = pattern_ref[k, half + fb, i]
                    for duo in range(duos):
                        fr = far_re[duo * rows : (duo + 1) * rows]
                        fi = far_im[duo * rows : (duo + 1) * rows]
                        re = near_re * fr + near_im * fi
                        im = near_im * fr - near_re * fi
                        if b:
                            re = acc[i, duo][0] + re
                            im = acc[i, duo][1] + im
                        acc[i, duo] = (re, im)
            for (i, duo), (re, im) in acc.items():
                lines[i, side, duo] = jnp.concatenate([re, im], axis=1)
        cross = jnp.concatenate([lines[key] for key in sorted(lines)], axis=0)
        top = cross.astype(jnp.bfloat16)
        rest = (cross - top.astype(jnp.float32)).astype(jnp.bfloat16)
        both = jnp.dot(jnp.concatenate([top, rest], axis=0), high_ref[fb], preferred_element_type=jnp.float32)
        size = cross.shape[0]
        total = total + (both[:size] + both[size:]) + jnp.dot(top, low_ref[fb], preferred_element_type=jnp.float32)
    for side in range(PADDED_LAGS // LANES):
        lag_ref[side] = total[:, side * LANES : (side + 1) * LANES]

    counts = {}
    for side in range(2):
        for b in range(groups):
            k = lax.bitwise_xor(swap, b)
            far = far_refs[side][b, blocks].astype(jnp.float32)
            for i in range(channels):
                near = pattern_ref[k, blocks, i]
                for duo in range(duos):
                    count = near * far[duo * rows : (duo + 1) * rows]
                    counts[i, side, duo] = counts[i, side, duo] + count if b else count
    pair_ref[...] = jnp.concatenate([counts[key] for key in sorted(counts)], axis=0)

    lines = channels * 2 * channels
    pairs = sum(pair_ref[pl.ds(s, lines, stride=windows), :] for s in range(windows))
    pairs = jnp.maximum(pairs, 1.0)
    parts = []
    for side in range(PADDED_LAGS // LANES):
        lag = sum(lag_ref[side, pl.ds(s, lines, stride=windows), :] for s in range(windows))
        parts.append(lag / pairs)
    result = jnp.concatenate(parts, axis=1)
    core = place_ref[1]
    for i in range(channels):
        block = result[i * 2 * channels : (i + 1) * 2 * channels]
        block = jnp.where(core == 0, block, pltpu.roll(block, channels, 0))
        out_ref[i] = block[:, :NUM_LAGS]


def correlate(place, near, far, channels, windows, tables):
    groups = len(near)
    blocks = near[0].shape[0]
    lines = channels * 2 * channels * windows
    vmem = pl.BlockSpec(memory_space=pltpu.VMEM)
    kernel = lambda *refs: correlate_kernel(groups, channels, windows, *refs)
    return pl.pallas_call(
        kernel,
        out_shape=jax.ShapeDtypeStruct((channels, 2 * channels, NUM_LAGS), jnp.float32),
        in_specs=[pl.BlockSpec(memory_space=pltpu.SMEM)] + [vmem] * (groups + 4),
        out_specs=vmem,
        scratch_shapes=[
            pltpu.VMEM((groups, blocks, channels, 2 * windows, LANES), jnp.float32),
            pltpu.VMEM((PADDED_LAGS // LANES, lines, LANES), jnp.float32),
            pltpu.VMEM((lines, LANES), jnp.float32),
        ],
        name="correlate",
    )(place, *near, *far, *tables)


def solution(mesh):
    groups = mesh.shape["tm"]
    assert mesh.shape["chan"] == CORES * groups and groups & (groups - 1) == 0

    def route(move):
        pairs = []
        for line in range(groups):
            for core in range(CORES):
                for t in range(groups):
                    to_line, to_core, to_t = move(line, core, t)
                    source = (line * CORES + core) * groups + t
                    pairs.append((source, (to_line * CORES + to_core) * groups + to_t))
        return pairs

    def send(value, move):
        return lax.ppermute(value, ("chan", "tm"), route(move))

    def local(spectra, keep_mask):
        channels, windows, width = spectra.shape
        own = whiten(spectra, keep_mask)
        far = [send(own, lambda line, core, t, b=b: (t ^ b, core, line)) for b in range(groups)]
        near = [own] + [send(own, lambda line, core, t, k=k: (line, core, t ^ k)) for k in range(1, groups)]
        *near, far = lax.optimization_barrier((*near, jnp.stack(far)))
        other = send(far, lambda line, core, t: (line, 1 - core, t))
        chan = lax.axis_index("chan")
        place = jnp.stack([(chan // CORES) ^ lax.axis_index("tm"), chan % CORES]).astype(jnp.int32)
        tables = [jnp.asarray(table) for table in lag_tables(width // 2)]
        return correlate(place, near, (far, other), channels, windows, tables)

    placed = (P("chan", "tm", None), P("chan", "tm"))
    return jax.shard_map(local, mesh=mesh, in_specs=placed, out_specs=P("chan", "tm", None), check_vma=False)
```

```python
import jax
import jax.numpy as jnp
import ml_dtypes
import numpy as np
from jax import lax
from jax.experimental import pallas as pl
from jax.experimental.pallas import tpu as pltpu
from jax.sharding import PartitionSpec as P

MAXLAG = 100
LANES = 128
CORES = 2
NUM_LAGS = 2 * MAXLAG + 1
PADDED_LAGS = 256
BEHIND = 0
VMEM_LIMIT = 32 << 20


def lag_table(nbins):
    freq = np.arange(nbins, dtype=np.int64) + 1
    shift = np.arange(NUM_LAGS, dtype=np.int64) - MAXLAG
    theta = (freq[:, None] * shift[None, :] % (2 * nbins)) * (np.pi / nbins)
    cosine = (np.cos(theta) / nbins).reshape(nbins // LANES, LANES, NUM_LAGS)
    sine = (-np.sin(theta) / nbins).reshape(nbins // LANES, LANES, NUM_LAGS)
    table = np.concatenate([cosine, sine], axis=1).astype(np.float32)
    table = np.pad(table, ((0, 0), (0, 0), (0, PADDED_LAGS - NUM_LAGS)))
    high = table.astype(ml_dtypes.bfloat16)
    low = (table - high.astype(np.float32)).astype(ml_dtypes.bfloat16)
    return np.stack([high, low], axis=1)


def whiten_kernel(mask_ref, spectra_ref, out_ref):
    channels, windows, width = spectra_ref.shape
    nbins = width // 2
    blocks = width // LANES
    row = lax.broadcasted_iota(jnp.int32, (windows, 1), 0)
    pieces = []
    masks = []
    for ch in range(channels):
        keep = jnp.zeros((windows, 1), jnp.float32)
        for s in range(windows):
            keep = jnp.where(row == s, mask_ref[ch, s].astype(jnp.float32), keep)
        spec = spectra_ref[ch]
        re = spec[:, :nbins]
        im = spec[:, nbins:]
        power = re * re + im * im
        level = jnp.mean(power, axis=-1, keepdims=True) + 1e-06
        factor = lax.rsqrt(power + 0.5 * level)
        pieces.append((re * factor * keep, im * factor * keep))
        masks.append(jnp.broadcast_to(keep, (windows, LANES)))
    re = jnp.concatenate([p[0] for p in pieces], axis=0).astype(jnp.bfloat16)
    im = jnp.concatenate([p[1] for p in pieces], axis=0).astype(jnp.bfloat16)
    half = blocks // 2
    for fb in range(half):
        out_ref[fb] = re[:, fb * LANES : (fb + 1) * LANES]
        out_ref[half + fb] = im[:, fb * LANES : (fb + 1) * LANES]
    out_ref[blocks] = jnp.concatenate(masks, axis=0).astype(jnp.bfloat16)


def whiten(spectra, keep_mask):
    channels, windows, width = spectra.shape
    return pl.pallas_call(
        whiten_kernel,
        out_shape=pltpu.VMEM((width // LANES + 1, channels * windows, LANES), jnp.bfloat16),
        in_specs=[pl.BlockSpec(memory_space=pltpu.SMEM), pl.BlockSpec(memory_space=pltpu.VMEM)],
        out_specs=pl.BlockSpec(memory_space=pltpu.VMEM),
        compiler_params=pltpu.CompilerParams(vmem_limit_bytes=VMEM_LIMIT),
        name="whiten",
    )(keep_mask, spectra)


def hold_kernel(table_ref, held_ref, arrived):
    fetches = [pltpu.make_async_copy(table_ref.at[n], held_ref.at[n], arrived.at[n]) for n in range(table_ref.shape[0])]
    for fetch in fetches:
        fetch.start()
    for fetch in fetches:
        fetch.wait()


def hold(table):
    return pl.pallas_call(
        hold_kernel,
        out_shape=pltpu.VMEM(table.shape, table.dtype),
        in_specs=[pl.BlockSpec(memory_space=pl.ANY)],
        out_specs=pl.BlockSpec(memory_space=pltpu.VMEM),
        scratch_shapes=[pltpu.SemaphoreType.DMA((table.shape[0],))],
        compiler_params=pltpu.CompilerParams(vmem_limit_bytes=VMEM_LIMIT),
        name="hold",
    )(table)


def exchange_plan(groups):
    far = [(("far", b), ("far", groups - 1 - b)) for b in range(groups // 2)]
    near = [(("near", k), ("near", groups - 1 - k)) for k in range(1, groups // 2)]
    return far + near + [(("near", groups - 1), ("near", groups - 1))]


def passes(blocks):
    return blocks[0] != blocks[1] or blocks[0][0] == "far"


def correlate_kernel(groups, channels, windows, *refs):
    plan = exchange_plan(groups)
    refs = list(refs)
    take = lambda count: [refs.pop(0) for _ in range(count)]
    (own_ref,), direct_refs = take(1), take(len(plan))
    passed_refs = {n: refs.pop(0) for n in range(len(plan)) if passes(plan[n])}
    held_ref, out_ref, pattern_ref, lag_ref, pair_ref = refs
    blocks = own_ref.shape[0] - 1
    half = blocks // 2
    duos = channels // 2
    rows = 2 * windows
    chan = lax.axis_index("chan")
    core = lax.rem(chan, CORES)
    swap = lax.bitwise_xor(lax.div(chan, CORES), lax.axis_index("tm"))

    wide = lambda ref: lambda fb: ref[fb].astype(jnp.float32)
    either = lambda ref, other: lambda fb: jnp.where(core == 0, ref[fb], other[fb]).astype(jnp.float32)
    near_loads = [(0, wide(own_ref))]
    upper = lax.broadcasted_iota(jnp.int32, (rows, LANES), 0) < windows
    far_loads = [[], []]
    for n, (block, other) in enumerate(plan):
        direct, passed = direct_refs[n], passed_refs.get(n)
        if block == other:
            if block[0] == "near":
                near_loads.append((block[1], wide(direct)))
            else:
                slot = lax.bitwise_xor(swap, block[1])
                far_loads[0].append((slot, wide(direct)))
                far_loads[1].append((slot, wide(passed)))
            continue
        turn = core * (block[1] ^ other[1])
        mine, theirs = lax.bitwise_xor(turn, block[1]), lax.bitwise_xor(turn, other[1])
        if block[0] == "near":
            near_loads += [(mine, wide(direct.at[0])), (theirs, wide(passed))]
        elif other[0] == "far":
            for side in range(2):
                far_loads[side].append((lax.bitwise_xor(swap, mine), wide(direct.at[side])))
                far_loads[side].append((lax.bitwise_xor(swap, theirs), wide(passed.at[1 - side])))
        else:
            near_loads.append((other[1], either(passed.at[1], direct.at[0])))
            for side in range(2):
                slot = lax.bitwise_xor(swap, block[1])
                far_loads[side].append((slot, either(direct.at[side], passed.at[1 - side])))

    for slot, load in near_loads:
        for fb in range(blocks + 1):
            block = load(fb)
            for duo in range(duos):
                tile = block[duo * rows : (duo + 1) * rows]
                turned = pltpu.roll(tile, windows, 0)
                pattern_ref[slot, fb, 2 * duo] = jnp.where(upper, tile, turned)
                pattern_ref[slot, fb, 2 * duo + 1] = jnp.where(upper, turned, tile)

    crosses = []

    def transform(fb):
        cross = crosses[fb]
        size = cross.shape[0]
        top = cross.astype(jnp.bfloat16)
        rest = (cross - top.astype(jnp.float32)).astype(jnp.bfloat16)
        both = jnp.dot(jnp.concatenate([top, rest], axis=0), held_ref[fb, 0], preferred_element_type=jnp.float32)
        return both[:size] + both[size:] + jnp.dot(top, held_ref[fb, 1], preferred_element_type=jnp.float32)

    total = jnp.zeros((channels * 2 * duos * rows, PADDED_LAGS), jnp.float32)
    for fb in range(half):
        lines = {}
        for side in range(2):
            acc = {}
            for n, (k, load) in enumerate(far_loads[side]):
                far_re = load(fb)
                far_im = load(half + fb)
                for i in range(channels):
                    near_re = pattern_ref[k, fb, i]
                    near_im = pattern_ref[k, half + fb, i]
                    for duo in range(duos):
                        fr = far_re[duo * rows : (duo + 1) * rows]
                        fi = far_im[duo * rows : (duo + 1) * rows]
                        re = near_re * fr + near_im * fi
                        im = near_im * fr - near_re * fi
                        if n:
                            re = acc[i, duo][0] + re
                            im = acc[i, duo][1] + im
                        acc[i, duo] = (re, im)
            for (i, duo), (re, im) in acc.items():
                lines[i, side, duo] = jnp.concatenate([re, im], axis=1)
        crosses.append(jnp.concatenate([lines[key] for key in sorted(lines)], axis=0))
        if fb >= BEHIND:
            total = total + transform(fb - BEHIND)
    for fb in range(half - BEHIND, half):
        total = total + transform(fb)
    for side in range(PADDED_LAGS // LANES):
        lag_ref[side] = total[:, side * LANES : (side + 1) * LANES]

    counts = {}
    for side in range(2):
        for n, (k, load) in enumerate(far_loads[side]):
            far = load(blocks)
            for i in range(channels):
                near = pattern_ref[k, blocks, i]
                for duo in range(duos):
                    count = near * far[duo * rows : (duo + 1) * rows]
                    counts[i, side, duo] = counts[i, side, duo] + count if n else count
    pair_ref[...] = jnp.concatenate([counts[key] for key in sorted(counts)], axis=0)

    lines = channels * 2 * channels
    pairs = sum(pair_ref[pl.ds(s, lines, stride=windows), :] for s in range(windows))
    pairs = jnp.maximum(pairs, 1.0)
    parts = []
    for side in range(PADDED_LAGS // LANES):
        lag = sum(lag_ref[side, pl.ds(s, lines, stride=windows), :] for s in range(windows))
        parts.append(lag / pairs)
    result = jnp.concatenate(parts, axis=1)
    for i in range(channels):
        block = result[i * 2 * channels : (i + 1) * 2 * channels]
        block = jnp.where(core == 0, block, pltpu.roll(block, channels, 0))
        out_ref[i] = block[:, :NUM_LAGS]


def correlate(groups, spectra, channels, windows, table):
    blocks = spectra[0].shape[0]
    lines = channels * 2 * channels * windows
    vmem = pl.BlockSpec(memory_space=pltpu.VMEM)
    kernel = lambda *refs: correlate_kernel(groups, channels, windows, *refs)
    held = [pltpu.with_memory_space_constraint(value, pltpu.VMEM) for value in (*spectra, table)]
    return pl.pallas_call(
        kernel,
        out_shape=jax.ShapeDtypeStruct((channels, 2 * channels, NUM_LAGS), jnp.float32),
        in_specs=[vmem] * len(held),
        out_specs=vmem,
        scratch_shapes=[
            pltpu.VMEM((groups, blocks, channels, 2 * windows, LANES), jnp.float32),
            pltpu.VMEM((PADDED_LAGS // LANES, lines, LANES), jnp.float32),
            pltpu.VMEM((lines, LANES), jnp.float32),
        ],
        compiler_params=pltpu.CompilerParams(vmem_limit_bytes=VMEM_LIMIT),
        name="correlate",
    )(*held)


def solution(mesh):
    groups = mesh.shape["tm"]
    assert mesh.shape["chan"] == CORES * groups and groups & (groups - 1) == 0

    def route(move):
        pairs = []
        for line in range(groups):
            for core in range(CORES):
                for t in range(groups):
                    to_line, to_core, to_t = move(line, core, t)
                    source = (line * CORES + core) * groups + t
                    pairs.append((source, (to_line * CORES + to_core) * groups + to_t))
        return pairs

    def send(value, move):
        return lax.ppermute(value, ("chan", "tm"), route(move))

    def local(spectra, keep_mask):
        channels, windows, width = spectra.shape
        swap = lambda value: send(value, lambda line, core, t: (line, 1 - core, t))
        swap = lambda value: send(value, lambda line, core, t: (line, 1 - core, t))
        moves = {
            "far": lambda line, core, t, b: (t ^ b, core, line),
            "near": lambda line, core, t, k: (line, core, t ^ k),
        }

        def fetch(value, *blocks):
            def move(line, core, t):
                kind, number = blocks[core]
                return moves[kind](line, core, t, number)

            return send(value, move)

        own = whiten(spectra, keep_mask)
        chip = jnp.stack([own, swap(own)])
        plan = exchange_plan(groups)
        direct = [fetch(own if blocks[0] == blocks[1] else chip, *blocks) for blocks in plan]
        passed = []
        for blocks, value in zip(plan, direct):
            if passes(blocks):
                half = blocks[0] != blocks[1] and blocks[0][0] == "near"
                passed.append(swap(value[1] if half else value))
        table = hold(jnp.asarray(lag_table(width // 2)))
        received = (own, *direct, *passed)
        return correlate(groups, received, channels, windows, table)

    placed = (P("chan", "tm", None), P("chan", "tm"))
    return jax.shard_map(local, mesh=mesh, in_specs=placed, out_specs=P("chan", "tm", None), check_vma=False)
```

```python
import jax
import jax.numpy as jnp
import ml_dtypes
import numpy as np
from jax import lax
from jax.experimental import pallas as pl
from jax.experimental.pallas import tpu as pltpu
from jax.sharding import PartitionSpec as P

MAXLAG = 100
LANES = 128
CORES = 2
NUM_LAGS = 2 * MAXLAG + 1
BLOCK = 2 * LANES
VMEM_LIMIT = 32 << 20


def lag_table(nbins):
    freq = np.arange(nbins, dtype=np.int64) + 1
    shift = np.arange(LANES, dtype=np.int64)
    theta = (freq[:, None] * shift[None, :] % (2 * nbins)) * (np.pi / nbins)
    used = shift[None, :] <= MAXLAG
    table = np.stack([np.where(used, turn(theta) / nbins, 0.0) for turn in (np.cos, np.sin)]).astype(np.float32)
    high = table.astype(ml_dtypes.bfloat16)
    low = (table - high.astype(np.float32)).astype(ml_dtypes.bfloat16)
    pair = np.concatenate([high, low], axis=-1).reshape(2, nbins // BLOCK, BLOCK, 2 * LANES)
    return pair.transpose(1, 0, 2, 3)


def in_hbm(value):
    return pltpu.with_memory_space_constraint(value, pltpu.HBM)


def whiten_kernel(mask_ref, spectra_ref, out_ref):
    channels, windows, width = spectra_ref.shape
    nbins = width // 2
    blocks = width // LANES
    row = lax.broadcasted_iota(jnp.int32, (windows, 1), 0)
    pieces = []
    masks = []
    for ch in range(channels):
        keep = jnp.zeros((windows, 1), jnp.float32)
        for s in range(windows):
            keep = jnp.where(row == s, mask_ref[ch, s].astype(jnp.float32), keep)
        spec = spectra_ref[ch]
        re = spec[:, :nbins]
        im = spec[:, nbins:]
        power = re * re + im * im
        level = jnp.mean(power, axis=-1, keepdims=True) + 1e-06
        factor = lax.rsqrt(power + 0.5 * level)
        pieces.append((re * factor * keep, im * factor * keep))
        masks.append(jnp.broadcast_to(keep, (windows, LANES)))
    re = jnp.concatenate([p[0] for p in pieces], axis=0).astype(jnp.bfloat16)
    im = jnp.concatenate([p[1] for p in pieces], axis=0).astype(jnp.bfloat16)
    half = blocks // 2
    for fb in range(half):
        out_ref[fb] = re[:, fb * LANES : (fb + 1) * LANES]
        out_ref[half + fb] = im[:, fb * LANES : (fb + 1) * LANES]
    out_ref[blocks] = jnp.concatenate(masks, axis=0).astype(jnp.bfloat16)


def whiten(spectra, keep_mask):
    channels, windows, width = spectra.shape
    return pl.pallas_call(
        whiten_kernel,
        out_shape=pltpu.VMEM((width // LANES + 1, channels * windows, LANES), jnp.bfloat16),
        in_specs=[pl.BlockSpec(memory_space=pltpu.SMEM), pl.BlockSpec(memory_space=pltpu.VMEM)],
        out_specs=pl.BlockSpec(memory_space=pltpu.VMEM),
        compiler_params=pltpu.CompilerParams(vmem_limit_bytes=VMEM_LIMIT),
        name="whiten",
    )(in_hbm(keep_mask), in_hbm(spectra))


def hold_kernel(table_ref, held_ref, arrived):
    fetches = [pltpu.make_async_copy(table_ref.at[n], held_ref.at[n], arrived.at[n]) for n in range(table_ref.shape[0])]
    for fetch in fetches:
        fetch.start()
    for fetch in fetches:
        fetch.wait()


def hold(table):
    return pl.pallas_call(
        hold_kernel,
        out_shape=pltpu.VMEM(table.shape, table.dtype),
        in_specs=[pl.BlockSpec(memory_space=pl.ANY)],
        out_specs=pl.BlockSpec(memory_space=pltpu.VMEM),
        scratch_shapes=[pltpu.SemaphoreType.DMA((table.shape[0],))],
        compiler_params=pltpu.CompilerParams(vmem_limit_bytes=VMEM_LIMIT),
        name="hold",
    )(in_hbm(table))


def exchange_plan(groups):
    far = [(("far", b), ("far", groups - 1 - b)) for b in range(groups // 2)]
    near = [(("near", k), ("near", groups - 1 - k)) for k in range(1, groups // 2)]
    return far + near + [(("near", groups - 1), ("near", groups - 1))]


def passes(blocks):
    return blocks[0] != blocks[1] or blocks[0][0] == "far"


def correlate_kernel(groups, channels, windows, *refs):
    plan = exchange_plan(groups)
    refs = list(refs)
    take = lambda count: [refs.pop(0) for _ in range(count)]
    (own_ref,), direct_refs = take(1), take(len(plan))
    passed_refs = {n: refs.pop(0) for n in range(len(plan)) if passes(plan[n])}
    held_ref, out_ref, pattern_ref, lag_ref, pair_ref = refs
    blocks = own_ref.shape[0] - 1
    half = blocks // 2
    duos = channels // 2
    rows = 2 * windows
    chan = lax.axis_index("chan")
    core = lax.rem(chan, CORES)
    swap = lax.bitwise_xor(lax.div(chan, CORES), lax.axis_index("tm"))

    wide = lambda ref: lambda fb: ref[fb].astype(jnp.float32)
    either = lambda ref, other: lambda fb: jnp.where(core == 0, ref[fb], other[fb]).astype(jnp.float32)
    near_loads = [(0, wide(own_ref))]
    upper = lax.broadcasted_iota(jnp.int32, (rows, LANES), 0) < windows
    far_loads = [[], []]
    for n, (block, other) in enumerate(plan):
        direct, passed = direct_refs[n], passed_refs.get(n)
        if block == other:
            if block[0] == "near":
                near_loads.append((block[1], wide(direct)))
            else:
                slot = lax.bitwise_xor(swap, block[1])
                far_loads[0].append((slot, wide(direct)))
                far_loads[1].append((slot, wide(passed)))
            continue
        turn = core * (block[1] ^ other[1])
        mine, theirs = lax.bitwise_xor(turn, block[1]), lax.bitwise_xor(turn, other[1])
        if block[0] == "near":
            near_loads += [(mine, wide(direct.at[0])), (theirs, wide(passed))]
        elif other[0] == "far":
            for side in range(2):
                far_loads[side].append((lax.bitwise_xor(swap, mine), wide(direct.at[side])))
                far_loads[side].append((lax.bitwise_xor(swap, theirs), wide(passed.at[1 - side])))
        else:
            near_loads.append((other[1], either(passed.at[1], direct.at[0])))
            for side in range(2):
                slot = lax.bitwise_xor(swap, block[1])
                far_loads[side].append((slot, either(direct.at[side], passed.at[1 - side])))

    for slot, load in near_loads:
        for fb in range(blocks + 1):
            block = load(fb)
            for duo in range(duos):
                tile = block[duo * rows : (duo + 1) * rows]
                turned = pltpu.roll(tile, windows, 0)
                pattern_ref[slot, fb, 2 * duo] = jnp.where(upper, tile, turned)
                pattern_ref[slot, fb, 2 * duo + 1] = jnp.where(upper, turned, tile)

    def transform(cross, part, p):
        size = cross.shape[0]
        top = cross.astype(jnp.bfloat16)
        rest = (cross - top.astype(jnp.float32)).astype(jnp.bfloat16)
        both = jnp.dot(jnp.concatenate([top, rest], axis=0), held_ref[p, part], preferred_element_type=jnp.float32)
        return both[:size, :LANES] + (both[:size, LANES:] + both[size:, :LANES])

    cosines = sines = None
    for p in range(half * LANES // BLOCK):
        lines = {}
        for fb in range(p * BLOCK // LANES, (p + 1) * BLOCK // LANES):
            for side in range(2):
                acc = {}
                for n, (k, load) in enumerate(far_loads[side]):
                    far_re = load(fb)
                    far_im = load(half + fb)
                    for i in range(channels):
                        near_re = pattern_ref[k, fb, i]
                        near_im = pattern_ref[k, half + fb, i]
                        for duo in range(duos):
                            fr = far_re[duo * rows : (duo + 1) * rows]
                            fi = far_im[duo * rows : (duo + 1) * rows]
                            re = near_re * fr + near_im * fi
                            im = near_im * fr - near_re * fi
                            if n:
                                re = acc[i, duo][0] + re
                                im = acc[i, duo][1] + im
                            acc[i, duo] = (re, im)
                for (i, duo), value in acc.items():
                    lines.setdefault((i, side, duo), []).append(value)
        for part in range(2):
            cross = jnp.concatenate(
                [jnp.concatenate([value[part] for value in lines[key]], axis=1) for key in sorted(lines)], axis=0
            )
            if part:
                sine = transform(cross, part, p)
            else:
                cosine = transform(cross, part, p)
        cosines = cosine if cosines is None else cosines + cosine
        sines = sine if sines is None else sines + sine
    lag_ref[0] = cosines
    lag_ref[1] = sines

    counts = {}
    for side in range(2):
        for n, (k, load) in enumerate(far_loads[side]):
            far = load(blocks)
            for i in range(channels):
                near = pattern_ref[k, blocks, i]
                for duo in range(duos):
                    count = near * far[duo * rows : (duo + 1) * rows]
                    counts[i, side, duo] = counts[i, side, duo] + count if n else count
    pair_ref[...] = jnp.concatenate([counts[key] for key in sorted(counts)], axis=0)

    lines = channels * 2 * channels
    pairs = sum(pair_ref[pl.ds(s, lines, stride=windows), :] for s in range(windows))
    pairs = jnp.maximum(pairs, 1.0)
    cosine = sum(lag_ref[0, pl.ds(s, lines, stride=windows), :] for s in range(windows))
    sine = sum(lag_ref[1, pl.ds(s, lines, stride=windows), :] for s in range(windows))
    ahead = (cosine - sine) / pairs
    behind = (cosine + sine) / pairs
    lane = lax.broadcasted_iota(jnp.int32, behind.shape, 1)
    behind = jnp.take_along_axis(behind, jnp.maximum(MAXLAG - lane, 0), axis=1)
    ahead = pltpu.roll(ahead, MAXLAG, 1)
    result = jnp.concatenate([jnp.where(lane < MAXLAG, behind, ahead), ahead], axis=1)
    for i in range(channels):
        block = result[i * 2 * channels : (i + 1) * 2 * channels]
        block = jnp.where(core == 0, block, pltpu.roll(block, channels, 0))
        out_ref[i] = block[:, :NUM_LAGS]


def correlate(groups, spectra, channels, windows, table):
    blocks = spectra[0].shape[0]
    lines = channels * 2 * channels * windows
    vmem = pl.BlockSpec(memory_space=pltpu.VMEM)
    kernel = lambda *refs: correlate_kernel(groups, channels, windows, *refs)
    held = [pltpu.with_memory_space_constraint(value, pltpu.VMEM) for value in (*spectra, table)]
    return pl.pallas_call(
        kernel,
        out_shape=jax.ShapeDtypeStruct((channels, 2 * channels, NUM_LAGS), jnp.float32),
        in_specs=[vmem] * len(held),
        out_specs=vmem,
        scratch_shapes=[
            pltpu.VMEM((groups, blocks, channels, 2 * windows, LANES), jnp.float32),
            pltpu.VMEM((2, lines, LANES), jnp.float32),
            pltpu.VMEM((lines, LANES), jnp.float32),
        ],
        compiler_params=pltpu.CompilerParams(vmem_limit_bytes=VMEM_LIMIT),
        name="correlate",
    )(*held)


def solution(mesh):
    groups = mesh.shape["tm"]
    assert mesh.shape["chan"] == CORES * groups and groups & (groups - 1) == 0

    def route(move):
        pairs = []
        for line in range(groups):
            for core in range(CORES):
                for t in range(groups):
                    to_line, to_core, to_t = move(line, core, t)
                    source = (line * CORES + core) * groups + t
                    pairs.append((source, (to_line * CORES + to_core) * groups + to_t))
        return pairs

    def send(value, move):
        return lax.ppermute(value, ("chan", "tm"), route(move))

    def local(spectra, keep_mask):
        channels, windows, width = spectra.shape
        swap = lambda value: send(value, lambda line, core, t: (line, 1 - core, t))
        swap = lambda value: send(value, lambda line, core, t: (line, 1 - core, t))
        moves = {
            "far": lambda line, core, t, b: (t ^ b, core, line),
            "near": lambda line, core, t, k: (line, core, t ^ k),
        }

        def fetch(value, *blocks):
            def move(line, core, t):
                kind, number = blocks[core]
                return moves[kind](line, core, t, number)

            return send(value, move)

        own = whiten(spectra, keep_mask)
        chip = jnp.stack([own, swap(own)])
        plan = exchange_plan(groups)
        direct = [fetch(own if blocks[0] == blocks[1] else chip, *blocks) for blocks in plan]
        passed = []
        for blocks, value in zip(plan, direct):
            if passes(blocks):
                half = blocks[0] != blocks[1] and blocks[0][0] == "near"
                passed.append(swap(value[1] if half else value))
        table = hold(jnp.asarray(lag_table(width // 2)))
        received = (own, *direct, *passed)
        return correlate(groups, received, channels, windows, table)

    placed = (P("chan", "tm", None), P("chan", "tm"))
    return jax.shard_map(local, mesh=mesh, in_specs=placed, out_specs=P("chan", "tm", None), check_vma=False)
```

```python
import jax
import jax.numpy as jnp
import ml_dtypes
import numpy as np
from jax import lax
from jax.experimental import pallas as pl
from jax.experimental.pallas import tpu as pltpu
from jax.sharding import PartitionSpec as P

MAXLAG = 100
LANES = 128
CORES = 2
NUM_LAGS = 2 * MAXLAG + 1
BLOCK = 2 * LANES
VMEM_LIMIT = 32 << 20


def lag_table(nbins):
    freq = np.arange(nbins, dtype=np.int64) + 1
    shift = np.arange(LANES, dtype=np.int64)
    theta = (freq[:, None] * shift[None, :] % (2 * nbins)) * (np.pi / nbins)
    used = shift[None, :] <= MAXLAG
    table = np.stack([np.where(used, turn(theta) / nbins, 0.0) for turn in (np.cos, np.sin)]).astype(np.float32)
    high = table.astype(ml_dtypes.bfloat16)
    low = (table - high.astype(np.float32)).astype(ml_dtypes.bfloat16)
    pair = np.concatenate([high, low], axis=-1).reshape(2, nbins // BLOCK, BLOCK, 2 * LANES)
    return pair.transpose(1, 0, 2, 3)


def in_hbm(value):
    return pltpu.with_memory_space_constraint(value, pltpu.HBM)


def whiten_into(out_ref, spectra_ref, mask_ref):
    channels, windows, width = spectra_ref.shape
    nbins = width // 2
    blocks = width // LANES
    shape = (windows, windows)
    diagonal = lax.broadcasted_iota(jnp.int32, shape, 0) == lax.broadcasted_iota(jnp.int32, shape, 1)
    pieces = []
    masks = []
    for ch in range(channels):
        keep = jnp.broadcast_to(mask_ref[ch : ch + 1].astype(jnp.float32), shape)
        keep = jnp.sum(jnp.where(diagonal, keep, 0.0), axis=1, keepdims=True)
        spec = spectra_ref[ch]
        re = spec[:, :nbins]
        im = spec[:, nbins:]
        power = re * re + im * im
        level = jnp.mean(power, axis=-1, keepdims=True) + 1e-06
        factor = lax.rsqrt(power + 0.5 * level)
        pieces.append((re * factor * keep, im * factor * keep))
        masks.append(jnp.broadcast_to(keep, (windows, LANES)))
    re = jnp.concatenate([p[0] for p in pieces], axis=0).astype(jnp.bfloat16)
    im = jnp.concatenate([p[1] for p in pieces], axis=0).astype(jnp.bfloat16)
    half = blocks // 2
    for fb in range(half):
        out_ref[fb] = re[:, fb * LANES : (fb + 1) * LANES]
        out_ref[half + fb] = im[:, fb * LANES : (fb + 1) * LANES]
    out_ref[blocks] = jnp.concatenate(masks, axis=0).astype(jnp.bfloat16)


def whiten_kernel(spectra_ref, mask_ref, table_ref, out_ref, held_ref, near_ref, kept_ref, arrived):
    spectra = pltpu.make_async_copy(spectra_ref, near_ref, arrived.at[0])
    table = pltpu.make_async_copy(table_ref, held_ref, arrived.at[1])
    mask = pltpu.make_async_copy(mask_ref, kept_ref, arrived.at[2])
    spectra.start()
    mask.start()
    table.start()
    mask.wait()
    spectra.wait()
    whiten_into(out_ref, near_ref, kept_ref)
    table.wait()


def whiten(spectra, keep_mask, table):
    channels, windows, width = spectra.shape
    vmem = pl.BlockSpec(memory_space=pltpu.VMEM)
    anywhere = pl.BlockSpec(memory_space=pl.ANY)
    return pl.pallas_call(
        whiten_kernel,
        out_shape=(
            pltpu.VMEM((width // LANES + 1, channels * windows, LANES), jnp.bfloat16),
            pltpu.VMEM(table.shape, table.dtype),
        ),
        in_specs=[anywhere] * 3,
        out_specs=(vmem, vmem),
        scratch_shapes=[
            pltpu.VMEM(spectra.shape, spectra.dtype),
            pltpu.VMEM(keep_mask.shape, keep_mask.dtype),
            pltpu.SemaphoreType.DMA((3,)),
        ],
        compiler_params=pltpu.CompilerParams(vmem_limit_bytes=VMEM_LIMIT),
        name="whiten",
    )(in_hbm(spectra), in_hbm(keep_mask), in_hbm(table))


def join_kernel(own_ref, spectra_ref, mask_ref, out_ref):
    out_ref[0] = own_ref[...]
    whiten_into(out_ref.at[1], spectra_ref, mask_ref)


def join(own, spectra, keep_mask):
    vmem = pl.BlockSpec(memory_space=pltpu.VMEM)
    held = [pltpu.with_memory_space_constraint(value, pltpu.VMEM) for value in (own, spectra, keep_mask)]
    return pl.pallas_call(
        join_kernel,
        out_shape=pltpu.VMEM((2, *own.shape), own.dtype),
        in_specs=[vmem] * 3,
        out_specs=vmem,
        compiler_params=pltpu.CompilerParams(vmem_limit_bytes=VMEM_LIMIT),
        name="join",
    )(*held)


def exchange_plan(groups):
    far = [(("far", b), ("far", groups - 1 - b)) for b in range(groups // 2)]
    near = [(("near", k), ("near", groups - 1 - k)) for k in range(1, groups // 2)]
    return far + near + [(("near", groups - 1), ("near", groups - 1))]


def passes(blocks):
    return blocks[0] != blocks[1] or blocks[0][0] == "far"


def correlate_kernel(groups, channels, windows, *refs):
    plan = exchange_plan(groups)
    refs = list(refs)
    take = lambda count: [refs.pop(0) for _ in range(count)]
    (own_ref,), direct_refs = take(1), take(len(plan))
    passed_refs = {n: refs.pop(0) for n in range(len(plan)) if passes(plan[n])}
    held_ref, out_ref, pattern_ref, cross_ref, pair_ref = refs
    blocks = own_ref.shape[0] - 1
    half = blocks // 2
    duos = channels // 2
    rows = 2 * windows
    chan = lax.axis_index("chan")
    core = lax.rem(chan, CORES)
    swap = lax.bitwise_xor(lax.div(chan, CORES), lax.axis_index("tm"))

    wide = lambda ref: lambda fb: ref[fb].astype(jnp.float32)
    either = lambda ref, other: lambda fb: jnp.where(core == 0, ref[fb], other[fb]).astype(jnp.float32)
    near_loads = [(0, wide(own_ref))]
    upper = lax.broadcasted_iota(jnp.int32, (rows, LANES), 0) < windows
    far_loads = [[], []]
    for n, (block, other) in enumerate(plan):
        direct, passed = direct_refs[n], passed_refs.get(n)
        if block == other:
            if block[0] == "near":
                near_loads.append((block[1], wide(direct)))
            else:
                slot = lax.bitwise_xor(swap, block[1])
                far_loads[0].append((slot, wide(direct)))
                far_loads[1].append((slot, wide(passed)))
            continue
        turn = core * (block[1] ^ other[1])
        mine, theirs = lax.bitwise_xor(turn, block[1]), lax.bitwise_xor(turn, other[1])
        if block[0] == "near":
            near_loads += [(mine, wide(direct.at[0])), (theirs, wide(passed))]
        elif other[0] == "far":
            for side in range(2):
                far_loads[side].append((lax.bitwise_xor(swap, mine), wide(direct.at[side])))
                far_loads[side].append((lax.bitwise_xor(swap, theirs), wide(passed.at[1 - side])))
        else:
            near_loads.append((other[1], either(passed.at[1], direct.at[0])))
            for side in range(2):
                slot = lax.bitwise_xor(swap, block[1])
                far_loads[side].append((slot, either(direct.at[side], passed.at[1 - side])))

    for slot, load in near_loads:
        for fb in range(blocks + 1):
            block = load(fb)
            for duo in range(duos):
                tile = block[duo * rows : (duo + 1) * rows]
                turned = pltpu.roll(tile, windows, 0)
                pattern_ref[slot, fb, 2 * duo] = jnp.where(upper, tile, turned)
                pattern_ref[slot, fb, 2 * duo + 1] = jnp.where(upper, turned, tile)

    def transform(cross, part, p):
        size = cross.shape[0]
        top = cross.astype(jnp.bfloat16)
        rest = (cross - top.astype(jnp.float32)).astype(jnp.bfloat16)
        both = jnp.dot(jnp.concatenate([top, rest], axis=0), held_ref[p, part], preferred_element_type=jnp.float32)
        return both[:size, :LANES] + (both[:size, LANES:] + both[size:, :LANES])

    lines = channels * 2 * channels
    cosine = sine = None
    for p in range(half * LANES // BLOCK):
        span = range(p * BLOCK // LANES, (p + 1) * BLOCK // LANES)
        for fb in span:
            for side in range(2):
                acc = {}
                for n, (k, load) in enumerate(far_loads[side]):
                    far_re = load(fb)
                    far_im = load(half + fb)
                    for i in range(channels):
                        near_re = pattern_ref[k, fb, i]
                        near_im = pattern_ref[k, half + fb, i]
                        for duo in range(duos):
                            fr = far_re[duo * rows : (duo + 1) * rows]
                            fi = far_im[duo * rows : (duo + 1) * rows]
                            re = near_re * fr + near_im * fi
                            im = near_im * fr - near_re * fi
                            if n:
                                re = acc[i, duo][0] + re
                                im = acc[i, duo][1] + im
                            acc[i, duo] = (re, im)
                for (i, duo), value in acc.items():
                    row = ((i * 2 + side) * duos + duo) * rows
                    for part in range(2):
                        cross_ref[part, fb, row : row + rows] = value[part]
        sums = []
        for part in range(2):
            cross = [
                sum(cross_ref[part, fb, pl.ds(s, lines, stride=windows), :] for s in range(windows)) for fb in span
            ]
            sums.append(transform(jnp.concatenate(cross, axis=1), part, p))
        cosine = sums[0] if p == 0 else cosine + sums[0]
        sine = sums[1] if p == 0 else sine + sums[1]

    counts = {}
    for side in range(2):
        for n, (k, load) in enumerate(far_loads[side]):
            far = load(blocks)
            for i in range(channels):
                near = pattern_ref[k, blocks, i]
                for duo in range(duos):
                    count = near * far[duo * rows : (duo + 1) * rows]
                    counts[i, side, duo] = counts[i, side, duo] + count if n else count
    pair_ref[...] = jnp.concatenate([counts[key] for key in sorted(counts)], axis=0)

    pairs = sum(pair_ref[pl.ds(s, lines, stride=windows), :] for s in range(windows))
    pairs = jnp.maximum(pairs, 1.0)
    ahead = (cosine - sine) / pairs
    behind = (cosine + sine) / pairs
    lane = lax.broadcasted_iota(jnp.int32, behind.shape, 1)
    behind = jnp.take_along_axis(behind, jnp.maximum(MAXLAG - lane, 0), axis=1)
    ahead = pltpu.roll(ahead, MAXLAG, 1)
    result = jnp.concatenate([jnp.where(lane < MAXLAG, behind, ahead), ahead], axis=1)
    for i in range(channels):
        block = result[i * 2 * channels : (i + 1) * 2 * channels]
        block = jnp.where(core == 0, block, pltpu.roll(block, channels, 0))
        out_ref[i] = block[:, :NUM_LAGS]


def correlate(groups, spectra, channels, windows, table):
    blocks = spectra[0].shape[0]
    lines = channels * 2 * channels * windows
    vmem = pl.BlockSpec(memory_space=pltpu.VMEM)
    kernel = lambda *refs: correlate_kernel(groups, channels, windows, *refs)
    held = [pltpu.with_memory_space_constraint(value, pltpu.VMEM) for value in (*spectra, table)]
    return pl.pallas_call(
        kernel,
        out_shape=jax.ShapeDtypeStruct((channels, 2 * channels, NUM_LAGS), jnp.float32),
        in_specs=[vmem] * len(held),
        out_specs=vmem,
        scratch_shapes=[
            pltpu.VMEM((groups, blocks, channels, 2 * windows, LANES), jnp.float32),
            pltpu.VMEM((2, blocks // 2, lines, LANES), jnp.float32),
            pltpu.VMEM((lines, LANES), jnp.float32),
        ],
        compiler_params=pltpu.CompilerParams(vmem_limit_bytes=VMEM_LIMIT),
        name="correlate",
    )(*held)


def solution(mesh):
    groups = mesh.shape["tm"]
    assert mesh.shape["chan"] == CORES * groups and groups & (groups - 1) == 0

    def route(move):
        pairs = []
        for line in range(groups):
            for core in range(CORES):
                for t in range(groups):
                    to_line, to_core, to_t = move(line, core, t)
                    source = (line * CORES + core) * groups + t
                    pairs.append((source, (to_line * CORES + to_core) * groups + to_t))
        return pairs

    def send(value, move):
        return lax.ppermute(value, ("chan", "tm"), route(move))

    def local(spectra, keep_mask):
        channels, windows, width = spectra.shape
        swap = lambda value: send(value, lambda line, core, t: (line, 1 - core, t))
        swap = lambda value: send(value, lambda line, core, t: (line, 1 - core, t))
        moves = {
            "far": lambda line, core, t, b: (t ^ b, core, line),
            "near": lambda line, core, t, k: (line, core, t ^ k),
        }

        def fetch(value, *blocks):
            def move(line, core, t):
                kind, number = blocks[core]
                return moves[kind](line, core, t, number)

            return send(value, move)

        sibling = swap(spectra), swap(keep_mask)
        own, table = whiten(spectra, keep_mask, jnp.asarray(lag_table(width // 2)))
        chip = join(own, *sibling)
        plan = exchange_plan(groups)
        direct = [fetch(own if blocks[0] == blocks[1] else chip, *blocks) for blocks in plan]
        passed = []
        for blocks, value in zip(plan, direct):
            if passes(blocks):
                half = blocks[0] != blocks[1] and blocks[0][0] == "near"
                passed.append(swap(value[1] if half else value))
        received = (own, *direct, *passed)
        return correlate(groups, received, channels, windows, table)

    placed = (P("chan", "tm", None), P("chan", "tm"))
    return jax.shard_map(local, mesh=mesh, in_specs=placed, out_specs=P("chan", "tm", None), check_vma=False)
```

```python
import jax
import jax.numpy as jnp
import ml_dtypes
import numpy as np
from jax import lax
from jax.experimental import pallas as pl
from jax.experimental.pallas import tpu as pltpu
from jax.sharding import PartitionSpec as P

MAXLAG = 100
LANES = 128
CORES = 2
NUM_LAGS = 2 * MAXLAG + 1
BLOCK = 2 * LANES
VMEM_LIMIT = 32 << 20


def lag_table(nbins):
    freq = np.arange(nbins, dtype=np.int64) + 1
    shift = np.arange(LANES, dtype=np.int64)
    theta = (freq[:, None] * shift[None, :] % (2 * nbins)) * (np.pi / nbins)
    used = shift[None, :] <= MAXLAG
    table = np.stack([np.where(used, turn(theta) / nbins, 0.0) for turn in (np.cos, np.sin)]).astype(np.float32)
    high = table.astype(ml_dtypes.bfloat16)
    low = (table - high.astype(np.float32)).astype(ml_dtypes.bfloat16)
    pair = np.concatenate([high, low], axis=-1).reshape(2, nbins // BLOCK, BLOCK, 2 * LANES)
    return pair.transpose(1, 0, 2, 3)


def in_hbm(value):
    return pltpu.with_memory_space_constraint(value, pltpu.HBM)


def whiten_into(out_ref, spectra_ref, mask_ref):
    channels, windows, width = spectra_ref.shape
    nbins = width // 2
    blocks = width // LANES
    shape = (windows, windows)
    diagonal = lax.broadcasted_iota(jnp.int32, shape, 0) == lax.broadcasted_iota(jnp.int32, shape, 1)
    pieces = []
    masks = []
    for ch in range(channels):
        keep = jnp.broadcast_to(mask_ref[ch : ch + 1].astype(jnp.float32), shape)
        keep = jnp.sum(jnp.where(diagonal, keep, 0.0), axis=1, keepdims=True)
        spec = spectra_ref[ch]
        re = spec[:, :nbins]
        im = spec[:, nbins:]
        power = re * re + im * im
        level = jnp.mean(power, axis=-1, keepdims=True) + 1e-06
        factor = lax.rsqrt(power + 0.5 * level)
        pieces.append((re * factor * keep, im * factor * keep))
        masks.append(jnp.broadcast_to(keep, (windows, LANES)))
    re = jnp.concatenate([p[0] for p in pieces], axis=0).astype(jnp.bfloat16)
    im = jnp.concatenate([p[1] for p in pieces], axis=0).astype(jnp.bfloat16)
    half = blocks // 2
    for fb in range(half):
        out_ref[fb] = re[:, fb * LANES : (fb + 1) * LANES]
        out_ref[half + fb] = im[:, fb * LANES : (fb + 1) * LANES]
    out_ref[blocks] = jnp.concatenate(masks, axis=0).astype(jnp.bfloat16)


def whiten_kernel(spectra_ref, mask_ref, table_ref, out_ref, held_ref, near_ref, kept_ref, arrived):
    spectra = pltpu.make_async_copy(spectra_ref, near_ref, arrived.at[0])
    table = pltpu.make_async_copy(table_ref, held_ref, arrived.at[1])
    mask = pltpu.make_async_copy(mask_ref, kept_ref, arrived.at[2])
    spectra.start()
    mask.start()
    table.start()
    mask.wait()
    spectra.wait()
    whiten_into(out_ref, near_ref, kept_ref)
    table.wait()


def whiten(spectra, keep_mask, table):
    channels, windows, width = spectra.shape
    vmem = pl.BlockSpec(memory_space=pltpu.VMEM)
    anywhere = pl.BlockSpec(memory_space=pl.ANY)
    return pl.pallas_call(
        whiten_kernel,
        out_shape=(
            pltpu.VMEM((width // LANES + 1, channels * windows, LANES), jnp.bfloat16),
            pltpu.VMEM(table.shape, table.dtype),
        ),
        in_specs=[anywhere] * 3,
        out_specs=(vmem, vmem),
        scratch_shapes=[
            pltpu.VMEM(spectra.shape, spectra.dtype),
            pltpu.VMEM(keep_mask.shape, keep_mask.dtype),
            pltpu.SemaphoreType.DMA((3,)),
        ],
        compiler_params=pltpu.CompilerParams(vmem_limit_bytes=VMEM_LIMIT),
        name="whiten",
    )(in_hbm(spectra), in_hbm(keep_mask), in_hbm(table))


def join_kernel(own_ref, spectra_ref, mask_ref, out_ref):
    out_ref[0] = own_ref[...]
    whiten_into(out_ref.at[1], spectra_ref, mask_ref)


def join(own, spectra, keep_mask):
    vmem = pl.BlockSpec(memory_space=pltpu.VMEM)
    held = [pltpu.with_memory_space_constraint(value, pltpu.VMEM) for value in (own, spectra, keep_mask)]
    return pl.pallas_call(
        join_kernel,
        out_shape=pltpu.VMEM((2, *own.shape), own.dtype),
        in_specs=[vmem] * 3,
        out_specs=vmem,
        compiler_params=pltpu.CompilerParams(vmem_limit_bytes=VMEM_LIMIT),
        name="join",
    )(*held)


def exchange_plan(groups):
    far = [(("far", b), ("far", groups - 1 - b)) for b in reversed(range(groups // 2))]
    near = [(("near", k), ("near", groups - 1 - k)) for k in range(1, groups // 2)]
    return far + near + [(("near", groups - 1), ("near", groups - 1))]


def place(groups):
    chan = lax.axis_index("chan")
    return lax.rem(chan, CORES), lax.bitwise_xor(lax.div(chan, CORES), lax.axis_index("tm"))


def slots(blocks, core, turn=0):
    mine = core * (blocks[0][1] ^ blocks[1][1])
    return [lax.bitwise_xor(lax.bitwise_xor(mine, block[1]), turn) for block in blocks]


def spread(blocks, pattern_ref):
    _, count, channels, rows, _ = pattern_ref.shape
    upper = lax.broadcasted_iota(jnp.int32, (rows, LANES), 0) < rows // 2
    for n, ref in enumerate(blocks):
        for fb in range(count):
            block = ref[fb].astype(jnp.float32)
            for duo in range(channels // 2):
                tile = block[duo * rows : (duo + 1) * rows]
                turned = pltpu.roll(tile, rows // 2, 0)
                pattern_ref[n, fb, 2 * duo] = jnp.where(upper, tile, turned)
                pattern_ref[n, fb, 2 * duo + 1] = jnp.where(upper, turned, tile)


def tally(slots, far_ref, pattern_ref, cross_ref, pair_ref):
    _, blocks, channels, rows, _ = pattern_ref.shape
    half = blocks // 2
    duos = channels // 2
    for fb in range(half):
        for side in range(2):
            acc = {}
            for n, slot in enumerate(slots):
                far_re = far_ref[slot, side, fb].astype(jnp.float32)
                far_im = far_ref[slot, side, half + fb].astype(jnp.float32)
                for i in range(channels):
                    near_re = pattern_ref[n, fb, i]
                    near_im = pattern_ref[n, half + fb, i]
                    for duo in range(duos):
                        fr = far_re[duo * rows : (duo + 1) * rows]
                        fi = far_im[duo * rows : (duo + 1) * rows]
                        re = near_re * fr + near_im * fi
                        im = near_im * fr - near_re * fi
                        if n:
                            re = acc[i, duo][0] + re
                            im = acc[i, duo][1] + im
                        acc[i, duo] = (re, im)
            for (i, duo), value in acc.items():
                row = ((i * 2 + side) * duos + duo) * rows
                for part in range(2):
                    cross_ref[part, fb, row : row + rows] = value[part]
    for side in range(2):
        acc = {}
        for n, slot in enumerate(slots):
            far = far_ref[slot, side, 2 * half].astype(jnp.float32)
            for i in range(channels):
                near = pattern_ref[n, 2 * half, i]
                for duo in range(duos):
                    count = near * far[duo * rows : (duo + 1) * rows]
                    acc[i, duo] = acc[i, duo] + count if n else count
        for (i, duo), value in acc.items():
            row = ((i * 2 + side) * duos + duo) * rows
            pair_ref[row : row + rows] = value


def over_windows(ref, windows):
    lines = ref.shape[0] // windows
    return sum(ref[pl.ds(s, lines, stride=windows), :] for s in range(windows))


def near_slots(groups, core, own):
    pairs = [slots(blocks, core) for blocks in exchange_plan(groups)[groups // 2 : -1]]
    return [0, *(mine for mine, _ in pairs)] if own else [groups - 1, *(theirs for _, theirs in pairs)]


def gather_kernel(groups, *refs):
    refs = list(refs)
    take = lambda count: [refs.pop(0) for _ in range(count)]
    near_refs, direct_refs, passed_refs = take(groups // 2), take(groups // 2), take(groups // 2)
    far_ref, part_ref, count_ref, pattern_ref, cross_ref, pair_ref = refs
    windows = pattern_ref.shape[3] // 2
    core, turn = place(groups)
    for blocks, direct, passed in zip(exchange_plan(groups), direct_refs, passed_refs):
        mine, theirs = slots(blocks, core, turn)
        for side in range(2):
            far_ref[mine, side] = direct[side]
            far_ref[theirs, side] = passed[1 - side]
    spread([near_refs[0], *(ref.at[0] for ref in near_refs[1:])], pattern_ref)
    tally(near_slots(groups, core, True), far_ref, pattern_ref, cross_ref, pair_ref)
    for part in range(2):
        for fb in range(cross_ref.shape[1]):
            part_ref[part, fb] = over_windows(cross_ref.at[part, fb], windows)
    count_ref[...] = over_windows(pair_ref, windows)


def finish_kernel(groups, *refs):
    late_refs = refs[: groups // 2]
    far_ref, part_ref, count_ref, held_ref, out_ref, pattern_ref, cross_ref, pair_ref = refs[groups // 2 :]
    channels = pattern_ref.shape[2]
    windows = pattern_ref.shape[3] // 2
    core, _ = place(groups)
    spread(late_refs, pattern_ref)
    tally(near_slots(groups, core, False), far_ref, pattern_ref, cross_ref, pair_ref)

    def transform(part, p):
        span = range(p * BLOCK // LANES, (p + 1) * BLOCK // LANES)
        cross = [part_ref[part, fb] + over_windows(cross_ref.at[part, fb], windows) for fb in span]
        cross = jnp.concatenate(cross, axis=1)
        size = cross.shape[0]
        top = cross.astype(jnp.bfloat16)
        rest = (cross - top.astype(jnp.float32)).astype(jnp.bfloat16)
        both = jnp.dot(jnp.concatenate([top, rest], axis=0), held_ref[p, part], preferred_element_type=jnp.float32)
        return both[:size, :LANES] + (both[:size, LANES:] + both[size:, :LANES])

    cosine, sine = [sum(transform(part, p) for p in range(held_ref.shape[0])) for part in range(2)]
    pairs = jnp.maximum(count_ref[...] + over_windows(pair_ref, windows), 1.0)
    ahead = (cosine - sine) / pairs
    behind = (cosine + sine) / pairs
    lane = lax.broadcasted_iota(jnp.int32, behind.shape, 1)
    behind = jnp.take_along_axis(behind, jnp.maximum(MAXLAG - lane, 0), axis=1)
    ahead = pltpu.roll(ahead, MAXLAG, 1)
    result = jnp.concatenate([jnp.where(lane < MAXLAG, behind, ahead), ahead], axis=1)
    for i in range(channels):
        block = result[i * 2 * channels : (i + 1) * 2 * channels]
        block = jnp.where(core == 0, block, pltpu.roll(block, channels, 0))
        out_ref[i] = block[:, :NUM_LAGS]


def correlate(groups, near, far, late, table, channels, windows):
    count = near[0].shape[0]
    lines = channels * 2 * channels
    vmem = pl.BlockSpec(memory_space=pltpu.VMEM)
    hold = lambda values: [pltpu.with_memory_space_constraint(value, pltpu.VMEM) for value in values]
    scratch = [
        pltpu.VMEM((groups // 2, count, channels, 2 * windows, LANES), jnp.float32),
        pltpu.VMEM((2, count // 2, lines * windows, LANES), jnp.float32),
        pltpu.VMEM((lines * windows, LANES), jnp.float32),
    ]
    sums = pl.pallas_call(
        lambda *refs: gather_kernel(groups, *refs),
        out_shape=(
            pltpu.VMEM((groups, 2, *near[0].shape), near[0].dtype),
            pltpu.VMEM((2, count // 2, lines, LANES), jnp.float32),
            pltpu.VMEM((lines, LANES), jnp.float32),
        ),
        in_specs=[vmem] * (len(near) + len(far)),
        out_specs=(vmem, vmem, vmem),
        scratch_shapes=scratch,
        compiler_params=pltpu.CompilerParams(vmem_limit_bytes=VMEM_LIMIT),
        name="gather",
    )(*hold((*near, *far)))
    return pl.pallas_call(
        lambda *refs: finish_kernel(groups, *refs),
        out_shape=jax.ShapeDtypeStruct((channels, 2 * channels, NUM_LAGS), jnp.float32),
        in_specs=[vmem] * (len(late) + 4),
        out_specs=vmem,
        scratch_shapes=scratch,
        compiler_params=pltpu.CompilerParams(vmem_limit_bytes=VMEM_LIMIT),
        name="finish",
    )(*hold((*late, *sums, table)))


def solution(mesh):
    groups = mesh.shape["tm"]
    assert mesh.shape["chan"] == CORES * groups and groups & (groups - 1) == 0

    def route(move):
        pairs = []
        for line in range(groups):
            for core in range(CORES):
                for t in range(groups):
                    to_line, to_core, to_t = move(line, core, t)
                    source = (line * CORES + core) * groups + t
                    pairs.append((source, (to_line * CORES + to_core) * groups + to_t))
        return pairs

    def send(value, move):
        return lax.ppermute(value, ("chan", "tm"), route(move))

    def local(spectra, keep_mask):
        channels, windows, width = spectra.shape
        swap = lambda value: send(value, lambda line, core, t: (line, 1 - core, t))
        moves = {
            "far": lambda line, core, t, b: (t ^ b, core, line),
            "near": lambda line, core, t, k: (line, core, t ^ k),
        }

        def fetch(value, *blocks):
            def move(line, core, t):
                kind, number = blocks[core]
                return moves[kind](line, core, t, number)

            return send(value, move)

        sibling = swap(spectra), swap(keep_mask)
        own, table = whiten(spectra, keep_mask, jnp.asarray(lag_table(width // 2)))
        chip = join(own, *sibling)
        plan = exchange_plan(groups)
        direct = [fetch(own if blocks[0] == blocks[1] else chip, *blocks) for blocks in plan]
        *direct, last = direct
        far, near = direct[: groups // 2], direct[groups // 2 :]
        far_passed = [swap(value) for value in far]
        late = [last, *(swap(value[1]) for value in near)]
        return correlate(groups, (own, *near), (*far, *far_passed), late, table, channels, windows)

    placed = (P("chan", "tm", None), P("chan", "tm"))
    return jax.shard_map(local, mesh=mesh, in_specs=placed, out_specs=P("chan", "tm", None), check_vma=False)
```

```python
import jax
import jax.numpy as jnp
import ml_dtypes
import numpy as np
from jax import lax
from jax.experimental import pallas as pl
from jax.experimental.pallas import tpu as pltpu
from jax.sharding import PartitionSpec as P

MAXLAG = 100
LANES = 128
CORES = 2
NUM_LAGS = 2 * MAXLAG + 1
BLOCK = 2 * LANES
VMEM_LIMIT = 32 << 20


def lag_table(nbins):
    freq = np.arange(nbins, dtype=np.int64) + 1
    shift = np.arange(LANES, dtype=np.int64)
    theta = (freq[:, None] * shift[None, :] % (2 * nbins)) * (np.pi / nbins)
    used = shift[None, :] <= MAXLAG
    table = np.stack([np.where(used, turn(theta) / nbins, 0.0) for turn in (np.cos, np.sin)]).astype(np.float32)
    high = table.astype(ml_dtypes.bfloat16)
    low = (table - high.astype(np.float32)).astype(ml_dtypes.bfloat16)
    pair = np.concatenate([high, low], axis=-1).reshape(2, nbins // BLOCK, BLOCK, 2 * LANES)
    return pair.transpose(1, 0, 2, 3)


def in_hbm(value):
    return pltpu.with_memory_space_constraint(value, pltpu.HBM)


def whiten_into(out_ref, spectra_ref, mask_ref):
    channels, windows, width = spectra_ref.shape
    nbins = width // 2
    blocks = width // LANES
    shape = (windows, windows)
    diagonal = lax.broadcasted_iota(jnp.int32, shape, 0) == lax.broadcasted_iota(jnp.int32, shape, 1)
    pieces = []
    masks = []
    for ch in range(channels):
        keep = jnp.broadcast_to(mask_ref[ch : ch + 1].astype(jnp.float32), shape)
        keep = jnp.sum(jnp.where(diagonal, keep, 0.0), axis=1, keepdims=True)
        spec = spectra_ref[ch]
        re = spec[:, :nbins]
        im = spec[:, nbins:]
        power = re * re + im * im
        level = jnp.mean(power, axis=-1, keepdims=True) + 1e-06
        factor = lax.rsqrt(power + 0.5 * level)
        pieces.append((re * factor * keep, im * factor * keep))
        masks.append(jnp.broadcast_to(keep, (windows, LANES)))
    re = jnp.concatenate([p[0] for p in pieces], axis=0).astype(jnp.bfloat16)
    im = jnp.concatenate([p[1] for p in pieces], axis=0).astype(jnp.bfloat16)
    half = blocks // 2
    for fb in range(half):
        out_ref[fb] = re[:, fb * LANES : (fb + 1) * LANES]
        out_ref[half + fb] = im[:, fb * LANES : (fb + 1) * LANES]
    out_ref[blocks] = jnp.concatenate(masks, axis=0).astype(jnp.bfloat16)


def whiten_kernel(spectra_ref, mask_ref, table_ref, out_ref, held_ref, near_ref, kept_ref, arrived):
    spectra = pltpu.make_async_copy(spectra_ref, near_ref, arrived.at[0])
    table = pltpu.make_async_copy(table_ref, held_ref, arrived.at[1])
    mask = pltpu.make_async_copy(mask_ref, kept_ref, arrived.at[2])
    spectra.start()
    mask.start()
    table.start()
    mask.wait()
    spectra.wait()
    whiten_into(out_ref, near_ref, kept_ref)
    table.wait()


def whiten(spectra, keep_mask, table):
    channels, windows, width = spectra.shape
    vmem = pl.BlockSpec(memory_space=pltpu.VMEM)
    anywhere = pl.BlockSpec(memory_space=pl.ANY)
    return pl.pallas_call(
        whiten_kernel,
        out_shape=(
            pltpu.VMEM((width // LANES + 1, channels * windows, LANES), jnp.bfloat16),
            pltpu.VMEM(table.shape, table.dtype),
        ),
        in_specs=[anywhere] * 3,
        out_specs=(vmem, vmem),
        scratch_shapes=[
            pltpu.VMEM(spectra.shape, spectra.dtype),
            pltpu.VMEM(keep_mask.shape, keep_mask.dtype),
            pltpu.SemaphoreType.DMA((3,)),
        ],
        compiler_params=pltpu.CompilerParams(vmem_limit_bytes=VMEM_LIMIT),
        name="whiten",
    )(in_hbm(spectra), in_hbm(keep_mask), in_hbm(table))


def join_kernel(own_ref, spectra_ref, mask_ref, out_ref):
    out_ref[0] = own_ref[...]
    whiten_into(out_ref.at[1], spectra_ref, mask_ref)


def join(own, spectra, keep_mask):
    vmem = pl.BlockSpec(memory_space=pltpu.VMEM)
    held = [pltpu.with_memory_space_constraint(value, pltpu.VMEM) for value in (own, spectra, keep_mask)]
    return pl.pallas_call(
        join_kernel,
        out_shape=pltpu.VMEM((2, *own.shape), own.dtype),
        in_specs=[vmem] * 3,
        out_specs=vmem,
        compiler_params=pltpu.CompilerParams(vmem_limit_bytes=VMEM_LIMIT),
        name="join",
    )(*held)


def exchange_plan(groups):
    quarter = groups // 4
    far = [(("far", b), ("far", b ^ 2 * quarter)) for b in range(quarter, 3 * quarter)]
    near = [(("near", groups - 1 - k), ("near", k)) for k in range(1, groups // 2)]
    return far + near + [(("near", groups - 1), ("near", groups - 1))]


def place(groups):
    chan = lax.axis_index("chan")
    return lax.rem(chan, CORES), lax.bitwise_xor(lax.div(chan, CORES), lax.axis_index("tm"))


def slots(blocks, core, turn=0):
    mine = core * (blocks[0][1] ^ blocks[1][1])
    return [lax.bitwise_xor(lax.bitwise_xor(mine, block[1]), turn) for block in blocks]


def spread(blocks, pattern_ref):
    _, count, channels, rows, _ = pattern_ref.shape
    upper = lax.broadcasted_iota(jnp.int32, (rows, LANES), 0) < rows // 2
    for n, ref in enumerate(blocks):
        for fb in range(count):
            block = ref[fb].astype(jnp.float32)
            for duo in range(channels // 2):
                tile = block[duo * rows : (duo + 1) * rows]
                turned = pltpu.roll(tile, rows // 2, 0)
                pattern_ref[n, fb, 2 * duo] = jnp.where(upper, tile, turned)
                pattern_ref[n, fb, 2 * duo + 1] = jnp.where(upper, turned, tile)


def tally(slots, far_ref, pattern_ref, cross_ref, pair_ref):
    _, blocks, channels, rows, _ = pattern_ref.shape
    half = blocks // 2
    duos = channels // 2
    for fb in range(half):
        for side in range(2):
            acc = {}
            for n, slot in enumerate(slots):
                far_re = far_ref[slot, side, fb].astype(jnp.float32)
                far_im = far_ref[slot, side, half + fb].astype(jnp.float32)
                for i in range(channels):
                    near_re = pattern_ref[n, fb, i]
                    near_im = pattern_ref[n, half + fb, i]
                    for duo in range(duos):
                        fr = far_re[duo * rows : (duo + 1) * rows]
                        fi = far_im[duo * rows : (duo + 1) * rows]
                        re = near_re * fr + near_im * fi
                        im = near_im * fr - near_re * fi
                        if n:
                            re = acc[i, duo][0] + re
                            im = acc[i, duo][1] + im
                        acc[i, duo] = (re, im)
            for (i, duo), value in acc.items():
                row = ((i * 2 + side) * duos + duo) * rows
                for part in range(2):
                    cross_ref[part, fb, row : row + rows] = value[part]
    for side in range(2):
        acc = {}
        for n, slot in enumerate(slots):
            far = far_ref[slot, side, 2 * half].astype(jnp.float32)
            for i in range(channels):
                near = pattern_ref[n, 2 * half, i]
                for duo in range(duos):
                    count = near * far[duo * rows : (duo + 1) * rows]
                    acc[i, duo] = acc[i, duo] + count if n else count
        for (i, duo), value in acc.items():
            row = ((i * 2 + side) * duos + duo) * rows
            pair_ref[row : row + rows] = value


def over_windows(ref, windows):
    lines = ref.shape[0] // windows
    return sum(ref[pl.ds(s, lines, stride=windows), :] for s in range(windows))


def near_slots(groups, core, own):
    pairs = [slots(blocks, core) for blocks in exchange_plan(groups)[groups // 2 : -1]]
    return [0, *(mine for mine, _ in pairs)] if own else [groups - 1, *(theirs for _, theirs in pairs)]


def gather_kernel(groups, *refs):
    refs = list(refs)
    take = lambda count: [refs.pop(0) for _ in range(count)]
    near_refs, direct_refs, passed_refs = take(groups // 2), take(groups // 2), take(groups // 2)
    far_ref, part_ref, count_ref, pattern_ref, cross_ref, pair_ref = refs
    windows = pattern_ref.shape[3] // 2
    core, turn = place(groups)
    for blocks, direct, passed in zip(exchange_plan(groups), direct_refs, passed_refs):
        mine, theirs = slots(blocks, core, turn)
        for side in range(2):
            far_ref[mine, side] = direct[side]
            far_ref[theirs, side] = passed[1 - side]
    spread([near_refs[0], *(ref.at[0] for ref in near_refs[1:])], pattern_ref)
    tally(near_slots(groups, core, True), far_ref, pattern_ref, cross_ref, pair_ref)
    for part in range(2):
        for fb in range(cross_ref.shape[1]):
            part_ref[part, fb] = over_windows(cross_ref.at[part, fb], windows)
    count_ref[...] = over_windows(pair_ref, windows)


def finish_kernel(groups, *refs):
    late_refs = refs[: groups // 2]
    far_ref, part_ref, count_ref, held_ref, out_ref, pattern_ref, cross_ref, pair_ref = refs[groups // 2 :]
    channels = pattern_ref.shape[2]
    windows = pattern_ref.shape[3] // 2
    core, _ = place(groups)
    spread(late_refs, pattern_ref)
    tally(near_slots(groups, core, False), far_ref, pattern_ref, cross_ref, pair_ref)

    def transform(part, p):
        span = range(p * BLOCK // LANES, (p + 1) * BLOCK // LANES)
        cross = [part_ref[part, fb] + over_windows(cross_ref.at[part, fb], windows) for fb in span]
        cross = jnp.concatenate(cross, axis=1)
        size = cross.shape[0]
        top = cross.astype(jnp.bfloat16)
        rest = (cross - top.astype(jnp.float32)).astype(jnp.bfloat16)
        both = jnp.dot(jnp.concatenate([top, rest], axis=0), held_ref[p, part], preferred_element_type=jnp.float32)
        return both[:size, :LANES] + (both[:size, LANES:] + both[size:, :LANES])

    cosine, sine = [sum(transform(part, p) for p in range(held_ref.shape[0])) for part in range(2)]
    pairs = jnp.maximum(count_ref[...] + over_windows(pair_ref, windows), 1.0)
    ahead = (cosine - sine) / pairs
    behind = (cosine + sine) / pairs
    lane = lax.broadcasted_iota(jnp.int32, behind.shape, 1)
    behind = jnp.take_along_axis(behind, jnp.maximum(MAXLAG - lane, 0), axis=1)
    ahead = pltpu.roll(ahead, MAXLAG, 1)
    result = jnp.concatenate([jnp.where(lane < MAXLAG, behind, ahead), ahead], axis=1)
    for i in range(channels):
        block = result[i * 2 * channels : (i + 1) * 2 * channels]
        block = jnp.where(core == 0, block, pltpu.roll(block, channels, 0))
        out_ref[i] = block[:, :NUM_LAGS]


def correlate(groups, near, far, late, table, channels, windows):
    count = near[0].shape[0]
    lines = channels * 2 * channels
    vmem = pl.BlockSpec(memory_space=pltpu.VMEM)
    hold = lambda values: [pltpu.with_memory_space_constraint(value, pltpu.VMEM) for value in values]
    scratch = [
        pltpu.VMEM((groups // 2, count, channels, 2 * windows, LANES), jnp.float32),
        pltpu.VMEM((2, count // 2, lines * windows, LANES), jnp.float32),
        pltpu.VMEM((lines * windows, LANES), jnp.float32),
    ]
    sums = pl.pallas_call(
        lambda *refs: gather_kernel(groups, *refs),
        out_shape=(
            pltpu.VMEM((groups, 2, *near[0].shape), near[0].dtype),
            pltpu.VMEM((2, count // 2, lines, LANES), jnp.float32),
            pltpu.VMEM((lines, LANES), jnp.float32),
        ),
        in_specs=[vmem] * (len(near) + len(far)),
        out_specs=(vmem, vmem, vmem),
        scratch_shapes=scratch,
        compiler_params=pltpu.CompilerParams(vmem_limit_bytes=VMEM_LIMIT),
        name="gather",
    )(*hold((*near, *far)))
    return pl.pallas_call(
        lambda *refs: finish_kernel(groups, *refs),
        out_shape=jax.ShapeDtypeStruct((channels, 2 * channels, NUM_LAGS), jnp.float32),
        in_specs=[vmem] * (len(late) + 4),
        out_specs=vmem,
        scratch_shapes=scratch,
        compiler_params=pltpu.CompilerParams(vmem_limit_bytes=VMEM_LIMIT),
        name="finish",
    )(*hold((*late, *sums, table)))


def solution(mesh):
    groups = mesh.shape["tm"]
    assert mesh.shape["chan"] == CORES * groups and groups & (groups - 1) == 0

    def route(move):
        pairs = []
        for line in range(groups):
            for core in range(CORES):
                for t in range(groups):
                    to_line, to_core, to_t = move(line, core, t)
                    source = (line * CORES + core) * groups + t
                    pairs.append((source, (to_line * CORES + to_core) * groups + to_t))
        return pairs

    def send(value, move):
        return lax.ppermute(value, ("chan", "tm"), route(move))

    def local(spectra, keep_mask):
        channels, windows, width = spectra.shape
        swap = lambda value: send(value, lambda line, core, t: (line, 1 - core, t))
        moves = {
            "far": lambda line, core, t, b: (t ^ b, core, line),
            "near": lambda line, core, t, k: (line, core, t ^ k),
        }

        def fetch(value, *blocks):
            def move(line, core, t):
                kind, number = blocks[core]
                return moves[kind](line, core, t, number)

            return send(value, move)

        sibling = swap(spectra), swap(keep_mask)
        own, table = whiten(spectra, keep_mask, jnp.asarray(lag_table(width // 2)))
        chip = join(own, *sibling)
        plan = exchange_plan(groups)
        direct = [fetch(own if blocks[0] == blocks[1] else chip, *blocks) for blocks in plan]
        *direct, last = direct
        far, near = direct[: groups // 2], direct[groups // 2 :]
        far_passed = [swap(value) for value in far]
        late = [last, *(swap(value[1]) for value in near)]
        return correlate(groups, (own, *near), (*far, *far_passed), late, table, channels, windows)

    placed = (P("chan", "tm", None), P("chan", "tm"))
    return jax.shard_map(local, mesh=mesh, in_specs=placed, out_specs=P("chan", "tm", None), check_vma=False)
```

```python
import jax
import jax.numpy as jnp
import ml_dtypes
import numpy as np
from jax import lax
from jax.experimental import pallas as pl
from jax.experimental.pallas import tpu as pltpu
from jax.sharding import PartitionSpec as P

MAXLAG = 100
LANES = 128
CORES = 2
NUM_LAGS = 2 * MAXLAG + 1
BLOCK = 2 * LANES
VMEM_LIMIT = 32 << 20


def lag_table(nbins):
    freq = np.arange(nbins, dtype=np.int64) + 1
    shift = np.arange(LANES, dtype=np.int64)
    theta = (freq[:, None] * shift[None, :] % (2 * nbins)) * (np.pi / nbins)
    used = shift[None, :] <= MAXLAG
    table = np.stack([np.where(used, turn(theta) / nbins, 0.0) for turn in (np.cos, np.sin)]).astype(np.float32)
    high = table.astype(ml_dtypes.bfloat16)
    low = (table - high.astype(np.float32)).astype(ml_dtypes.bfloat16)
    pair = np.concatenate([high, low], axis=-1).reshape(2, nbins // BLOCK, BLOCK, 2 * LANES)
    return pair.transpose(1, 0, 2, 3)


def in_hbm(value):
    return pltpu.with_memory_space_constraint(value, pltpu.HBM)


def whiten_into(out_ref, spectra_ref, mask_ref):
    channels, windows, width = spectra_ref.shape
    nbins = width // 2
    blocks = width // LANES
    shape = (windows, windows)
    diagonal = lax.broadcasted_iota(jnp.int32, shape, 0) == lax.broadcasted_iota(jnp.int32, shape, 1)
    pieces = []
    masks = []
    for ch in range(channels):
        keep = jnp.broadcast_to(mask_ref[ch : ch + 1].astype(jnp.float32), shape)
        keep = jnp.sum(jnp.where(diagonal, keep, 0.0), axis=1, keepdims=True)
        spec = spectra_ref[ch]
        re = spec[:, :nbins]
        im = spec[:, nbins:]
        power = re * re + im * im
        level = jnp.mean(power, axis=-1, keepdims=True) + 1e-06
        factor = lax.rsqrt(power + 0.5 * level)
        pieces.append((re * factor * keep, im * factor * keep))
        masks.append(jnp.broadcast_to(keep, (windows, LANES)))
    re = jnp.concatenate([p[0] for p in pieces], axis=0).astype(jnp.bfloat16)
    im = jnp.concatenate([p[1] for p in pieces], axis=0).astype(jnp.bfloat16)
    half = blocks // 2
    for fb in range(half):
        out_ref[fb] = re[:, fb * LANES : (fb + 1) * LANES]
        out_ref[half + fb] = im[:, fb * LANES : (fb + 1) * LANES]
    out_ref[blocks] = jnp.concatenate(masks, axis=0).astype(jnp.bfloat16)


def whiten_kernel(spectra_ref, mask_ref, table_ref, out_ref, held_ref, near_ref, kept_ref, arrived):
    spectra = pltpu.make_async_copy(spectra_ref, near_ref, arrived.at[0])
    table = pltpu.make_async_copy(table_ref, held_ref, arrived.at[1])
    mask = pltpu.make_async_copy(mask_ref, kept_ref, arrived.at[2])
    spectra.start()
    mask.start()
    table.start()
    mask.wait()
    spectra.wait()
    whiten_into(out_ref, near_ref, kept_ref)
    table.wait()


def whiten(spectra, keep_mask, table):
    channels, windows, width = spectra.shape
    vmem = pl.BlockSpec(memory_space=pltpu.VMEM)
    anywhere = pl.BlockSpec(memory_space=pl.ANY)
    return pl.pallas_call(
        whiten_kernel,
        out_shape=(
            pltpu.VMEM((width // LANES + 1, channels * windows, LANES), jnp.bfloat16),
            pltpu.VMEM(table.shape, table.dtype),
        ),
        in_specs=[anywhere] * 3,
        out_specs=(vmem, vmem),
        scratch_shapes=[
            pltpu.VMEM(spectra.shape, spectra.dtype),
            pltpu.VMEM(keep_mask.shape, keep_mask.dtype),
            pltpu.SemaphoreType.DMA((3,)),
        ],
        compiler_params=pltpu.CompilerParams(vmem_limit_bytes=VMEM_LIMIT),
        name="whiten",
    )(in_hbm(spectra), in_hbm(keep_mask), in_hbm(table))


def join_kernel(own_ref, spectra_ref, mask_ref, out_ref):
    out_ref[0] = own_ref[...]
    whiten_into(out_ref.at[1], spectra_ref, mask_ref)


def join(own, spectra, keep_mask):
    vmem = pl.BlockSpec(memory_space=pltpu.VMEM)
    held = [pltpu.with_memory_space_constraint(value, pltpu.VMEM) for value in (own, spectra, keep_mask)]
    return pl.pallas_call(
        join_kernel,
        out_shape=pltpu.VMEM((2, *own.shape), own.dtype),
        in_specs=[vmem] * 3,
        out_specs=vmem,
        compiler_params=pltpu.CompilerParams(vmem_limit_bytes=VMEM_LIMIT),
        name="join",
    )(*held)


def exchange_plan(groups):
    quarter = groups // 4
    far = [(("far", b), ("far", b ^ 2 * quarter)) for b in range(quarter, 3 * quarter)]
    near = [(("near", groups - 1 - k), ("near", k)) for k in range(1, groups // 2)]
    return far + near + [(("near", groups - 1), ("near", groups - 1))]


def place(groups):
    chan = lax.axis_index("chan")
    return lax.rem(chan, CORES), lax.bitwise_xor(lax.div(chan, CORES), lax.axis_index("tm"))


def slots(blocks, core, turn=0):
    mine = core * (blocks[0][1] ^ blocks[1][1])
    return [lax.bitwise_xor(lax.bitwise_xor(mine, block[1]), turn) for block in blocks]


def spread(blocks, pattern_ref):
    _, count, channels, rows, _ = pattern_ref.shape
    upper = lax.broadcasted_iota(jnp.int32, (rows, LANES), 0) < rows // 2
    for n, ref in enumerate(blocks):
        for fb in range(count):
            block = ref[fb].astype(jnp.float32)
            for duo in range(channels // 2):
                tile = block[duo * rows : (duo + 1) * rows]
                turned = pltpu.roll(tile, rows // 2, 0)
                pattern_ref[n, fb, 2 * duo] = jnp.where(upper, tile, turned)
                pattern_ref[n, fb, 2 * duo + 1] = jnp.where(upper, turned, tile)


def tally(slots, far_ref, pattern_ref, cross_ref, span):
    _, blocks, channels, rows, _ = pattern_ref.shape
    half = blocks // 2
    duos = channels // 2
    for fb in span:
        for side in range(2):
            acc = {}
            for n, slot in enumerate(slots):
                far_re = far_ref[slot, side, fb].astype(jnp.float32)
                far_im = far_ref[slot, side, half + fb].astype(jnp.float32)
                for i in range(channels):
                    near_re = pattern_ref[n, fb, i]
                    near_im = pattern_ref[n, half + fb, i]
                    for duo in range(duos):
                        fr = far_re[duo * rows : (duo + 1) * rows]
                        fi = far_im[duo * rows : (duo + 1) * rows]
                        re = near_re * fr + near_im * fi
                        im = near_im * fr - near_re * fi
                        if n:
                            re = acc[i, duo][0] + re
                            im = acc[i, duo][1] + im
                        acc[i, duo] = (re, im)
            for (i, duo), value in acc.items():
                row = ((i * 2 + side) * duos + duo) * rows
                for part in range(2):
                    cross_ref[part, fb, row : row + rows] = value[part]


def tally_kept(slots, far_ref, pattern_ref, pair_ref):
    _, blocks, channels, rows, _ = pattern_ref.shape
    half = blocks // 2
    duos = channels // 2
    for side in range(2):
        acc = {}
        for n, slot in enumerate(slots):
            far = far_ref[slot, side, 2 * half].astype(jnp.float32)
            for i in range(channels):
                near = pattern_ref[n, 2 * half, i]
                for duo in range(duos):
                    count = near * far[duo * rows : (duo + 1) * rows]
                    acc[i, duo] = acc[i, duo] + count if n else count
        for (i, duo), value in acc.items():
            row = ((i * 2 + side) * duos + duo) * rows
            pair_ref[row : row + rows] = value


def over_windows(ref, windows):
    lines = ref.shape[0] // windows
    return sum(ref[pl.ds(s, lines, stride=windows), :] for s in range(windows))


def near_slots(groups, core, own):
    pairs = [slots(blocks, core) for blocks in exchange_plan(groups)[groups // 2 : -1]]
    return [0, *(mine for mine, _ in pairs)] if own else [groups - 1, *(theirs for _, theirs in pairs)]


def gather_kernel(groups, *refs):
    refs = list(refs)
    take = lambda count: [refs.pop(0) for _ in range(count)]
    near_refs, direct_refs, passed_refs = take(groups // 2), take(groups // 2), take(groups // 2)
    far_ref, part_ref, count_ref, pattern_ref, cross_ref, pair_ref = refs
    windows = pattern_ref.shape[3] // 2
    core, turn = place(groups)
    for blocks, direct, passed in zip(exchange_plan(groups), direct_refs, passed_refs):
        mine, theirs = slots(blocks, core, turn)
        for side in range(2):
            far_ref[mine, side] = direct[side]
            far_ref[theirs, side] = passed[1 - side]
    spread([near_refs[0], *(ref.at[0] for ref in near_refs[1:])], pattern_ref)
    own = near_slots(groups, core, True)
    tally(own, far_ref, pattern_ref, cross_ref, range(cross_ref.shape[1]))
    tally_kept(own, far_ref, pattern_ref, pair_ref)
    for part in range(2):
        for fb in range(cross_ref.shape[1]):
            part_ref[part, fb] = over_windows(cross_ref.at[part, fb], windows)
    count_ref[...] = over_windows(pair_ref, windows)


def finish_kernel(groups, *refs):
    late_refs = refs[: groups // 2]
    far_ref, part_ref, count_ref, held_ref, out_ref, pattern_ref, cross_ref, pair_ref = refs[groups // 2 :]
    channels = pattern_ref.shape[2]
    windows = pattern_ref.shape[3] // 2
    core, _ = place(groups)
    spread(late_refs, pattern_ref)
    brought = near_slots(groups, core, False)
    tally_kept(brought, far_ref, pattern_ref, pair_ref)

    def transform(part, p):
        span = range(p * BLOCK // LANES, (p + 1) * BLOCK // LANES)
        cross = [part_ref[part, fb] + over_windows(cross_ref.at[part, fb], windows) for fb in span]
        cross = jnp.concatenate(cross, axis=1)
        size = cross.shape[0]
        top = cross.astype(jnp.bfloat16)
        rest = (cross - top.astype(jnp.float32)).astype(jnp.bfloat16)
        both = jnp.dot(jnp.concatenate([top, rest], axis=0), held_ref[p, part], preferred_element_type=jnp.float32)
        return both[:size, :LANES] + (both[:size, LANES:] + both[size:, :LANES])

    sums = []
    for p in range(held_ref.shape[0]):
        span = range(p * BLOCK // LANES, (p + 1) * BLOCK // LANES)
        tally(brought, far_ref, pattern_ref, cross_ref, span)
        if p:
            sums.append([transform(part, p - 1) for part in range(2)])
    sums.append([transform(part, p) for part in range(2)])
    cosine, sine = [sum(parts) for parts in zip(*sums)]
    pairs = jnp.maximum(count_ref[...] + over_windows(pair_ref, windows), 1.0)
    ahead = (cosine - sine) / pairs
    behind = (cosine + sine) / pairs
    lane = lax.broadcasted_iota(jnp.int32, behind.shape, 1)
    behind = jnp.take_along_axis(behind, jnp.maximum(MAXLAG - lane, 0), axis=1)
    ahead = pltpu.roll(ahead, MAXLAG, 1)
    result = jnp.concatenate([jnp.where(lane < MAXLAG, behind, ahead), ahead], axis=1)
    for i in range(channels):
        block = result[i * 2 * channels : (i + 1) * 2 * channels]
        block = jnp.where(core == 0, block, pltpu.roll(block, channels, 0))
        out_ref[i] = block[:, :NUM_LAGS]


def correlate(groups, near, far, late, table, channels, windows):
    count = near[0].shape[0]
    lines = channels * 2 * channels
    vmem = pl.BlockSpec(memory_space=pltpu.VMEM)
    hold = lambda values: [pltpu.with_memory_space_constraint(value, pltpu.VMEM) for value in values]
    scratch = [
        pltpu.VMEM((groups // 2, count, channels, 2 * windows, LANES), jnp.float32),
        pltpu.VMEM((2, count // 2, lines * windows, LANES), jnp.float32),
        pltpu.VMEM((lines * windows, LANES), jnp.float32),
    ]
    sums = pl.pallas_call(
        lambda *refs: gather_kernel(groups, *refs),
        out_shape=(
            pltpu.VMEM((groups, 2, *near[0].shape), near[0].dtype),
            pltpu.VMEM((2, count // 2, lines, LANES), jnp.float32),
            pltpu.VMEM((lines, LANES), jnp.float32),
        ),
        in_specs=[vmem] * (len(near) + len(far)),
        out_specs=(vmem, vmem, vmem),
        scratch_shapes=scratch,
        compiler_params=pltpu.CompilerParams(vmem_limit_bytes=VMEM_LIMIT),
        name="gather",
    )(*hold((*near, *far)))
    return pl.pallas_call(
        lambda *refs: finish_kernel(groups, *refs),
        out_shape=jax.ShapeDtypeStruct((channels, 2 * channels, NUM_LAGS), jnp.float32),
        in_specs=[vmem] * (len(late) + 4),
        out_specs=vmem,
        scratch_shapes=scratch,
        compiler_params=pltpu.CompilerParams(vmem_limit_bytes=VMEM_LIMIT),
        name="finish",
    )(*hold((*late, *sums, table)))


def solution(mesh):
    groups = mesh.shape["tm"]
    assert mesh.shape["chan"] == CORES * groups and groups & (groups - 1) == 0

    def route(move):
        pairs = []
        for line in range(groups):
            for core in range(CORES):
                for t in range(groups):
                    to_line, to_core, to_t = move(line, core, t)
                    source = (line * CORES + core) * groups + t
                    pairs.append((source, (to_line * CORES + to_core) * groups + to_t))
        return pairs

    def send(value, move):
        return lax.ppermute(value, ("chan", "tm"), route(move))

    def local(spectra, keep_mask):
        channels, windows, width = spectra.shape
        swap = lambda value: send(value, lambda line, core, t: (line, 1 - core, t))
        moves = {
            "far": lambda line, core, t, b: (t ^ b, core, line),
            "near": lambda line, core, t, k: (line, core, t ^ k),
        }

        def fetch(value, *blocks):
            def move(line, core, t):
                kind, number = blocks[core]
                return moves[kind](line, core, t, number)

            return send(value, move)

        sibling = swap(spectra), swap(keep_mask)
        own, table = whiten(spectra, keep_mask, jnp.asarray(lag_table(width // 2)))
        chip = join(own, *sibling)
        plan = exchange_plan(groups)
        direct = [fetch(own if blocks[0] == blocks[1] else chip, *blocks) for blocks in plan]
        *direct, last = direct
        far, near = direct[: groups // 2], direct[groups // 2 :]
        far_passed = [swap(value) for value in far]
        late = [last, *(swap(value[1]) for value in near)]
        return correlate(groups, (own, *near), (*far, *far_passed), late, table, channels, windows)

    placed = (P("chan", "tm", None), P("chan", "tm"))
    return jax.shard_map(local, mesh=mesh, in_specs=placed, out_specs=P("chan", "tm", None), check_vma=False)
```

```python
import jax
import jax.numpy as jnp
import ml_dtypes
import numpy as np
from jax import lax
from jax.experimental import pallas as pl
from jax.experimental.pallas import tpu as pltpu
from jax.sharding import PartitionSpec as P

MAXLAG = 100
LANES = 128
CORES = 2
NUM_LAGS = 2 * MAXLAG + 1
BLOCK = 2 * LANES
VMEM_LIMIT = 32 << 20


def lag_table(nbins):
    freq = np.arange(nbins, dtype=np.int64) + 1
    shift = np.arange(LANES, dtype=np.int64)
    theta = (freq[:, None] * shift[None, :] % (2 * nbins)) * (np.pi / nbins)
    used = shift[None, :] <= MAXLAG
    table = np.stack([np.where(used, turn(theta) / nbins, 0.0) for turn in (np.cos, np.sin)]).astype(np.float32)
    high = table.astype(ml_dtypes.bfloat16)
    low = (table - high.astype(np.float32)).astype(ml_dtypes.bfloat16)
    pair = np.concatenate([high, low], axis=-1).reshape(2, nbins // BLOCK, BLOCK, 2 * LANES)
    return pair.transpose(1, 0, 2, 3)


def in_hbm(value):
    return pltpu.with_memory_space_constraint(value, pltpu.HBM)


def whiten_into(out_ref, spectra_ref, mask_ref):
    channels, windows, width = spectra_ref.shape
    nbins = width // 2
    blocks = width // LANES
    shape = (windows, windows)
    diagonal = lax.broadcasted_iota(jnp.int32, shape, 0) == lax.broadcasted_iota(jnp.int32, shape, 1)
    pieces = []
    masks = []
    for ch in range(channels):
        keep = jnp.broadcast_to(mask_ref[ch : ch + 1].astype(jnp.float32), shape)
        keep = jnp.sum(jnp.where(diagonal, keep, 0.0), axis=1, keepdims=True)
        spec = spectra_ref[ch]
        re = spec[:, :nbins]
        im = spec[:, nbins:]
        power = re * re + im * im
        level = jnp.mean(power, axis=-1, keepdims=True) + 1e-06
        factor = lax.rsqrt(power + 0.5 * level)
        pieces.append((re * factor * keep, im * factor * keep))
        masks.append(jnp.broadcast_to(keep, (windows, LANES)))
    re = jnp.concatenate([p[0] for p in pieces], axis=0).astype(jnp.bfloat16)
    im = jnp.concatenate([p[1] for p in pieces], axis=0).astype(jnp.bfloat16)
    half = blocks // 2
    for fb in range(half):
        out_ref[fb] = re[:, fb * LANES : (fb + 1) * LANES]
        out_ref[half + fb] = im[:, fb * LANES : (fb + 1) * LANES]
    out_ref[blocks] = jnp.concatenate(masks, axis=0).astype(jnp.bfloat16)


def whiten_kernel(spectra_ref, mask_ref, table_ref, out_ref, held_ref, near_ref, kept_ref, arrived):
    spectra = pltpu.make_async_copy(spectra_ref, near_ref, arrived.at[0])
    table = pltpu.make_async_copy(table_ref, held_ref, arrived.at[1])
    mask = pltpu.make_async_copy(mask_ref, kept_ref, arrived.at[2])
    spectra.start()
    mask.start()
    table.start()
    mask.wait()
    spectra.wait()
    whiten_into(out_ref, near_ref, kept_ref)
    table.wait()


def whiten(spectra, keep_mask, table):
    channels, windows, width = spectra.shape
    vmem = pl.BlockSpec(memory_space=pltpu.VMEM)
    anywhere = pl.BlockSpec(memory_space=pl.ANY)
    return pl.pallas_call(
        whiten_kernel,
        out_shape=(
            pltpu.VMEM((width // LANES + 1, channels * windows, LANES), jnp.bfloat16),
            pltpu.VMEM(table.shape, table.dtype),
        ),
        in_specs=[anywhere] * 3,
        out_specs=(vmem, vmem),
        scratch_shapes=[
            pltpu.VMEM(spectra.shape, spectra.dtype),
            pltpu.VMEM(keep_mask.shape, keep_mask.dtype),
            pltpu.SemaphoreType.DMA((3,)),
        ],
        compiler_params=pltpu.CompilerParams(vmem_limit_bytes=VMEM_LIMIT),
        name="whiten",
    )(in_hbm(spectra), in_hbm(keep_mask), in_hbm(table))


def join_kernel(own_ref, spectra_ref, mask_ref, out_ref):
    out_ref[0] = own_ref[...]
    whiten_into(out_ref.at[1], spectra_ref, mask_ref)


def join(own, spectra, keep_mask):
    vmem = pl.BlockSpec(memory_space=pltpu.VMEM)
    held = [pltpu.with_memory_space_constraint(value, pltpu.VMEM) for value in (own, spectra, keep_mask)]
    return pl.pallas_call(
        join_kernel,
        out_shape=pltpu.VMEM((2, *own.shape), own.dtype),
        in_specs=[vmem] * 3,
        out_specs=vmem,
        compiler_params=pltpu.CompilerParams(vmem_limit_bytes=VMEM_LIMIT),
        name="join",
    )(*held)


def exchange_plan(groups):
    quarter = groups // 4
    far = [(("far", b), ("far", b ^ 2 * quarter)) for b in range(quarter, 3 * quarter)]
    near = [(("near", groups - 1 - k), ("near", k)) for k in range(1, groups // 2)]
    return far + near + [(("near", groups - 1), ("near", groups - 1))]


def place(groups):
    chan = lax.axis_index("chan")
    return lax.rem(chan, CORES), lax.bitwise_xor(lax.div(chan, CORES), lax.axis_index("tm"))


def slots(blocks, core, turn=0):
    mine = core * (blocks[0][1] ^ blocks[1][1])
    return [lax.bitwise_xor(lax.bitwise_xor(mine, block[1]), turn) for block in blocks]


def spread(blocks, pattern_ref):
    _, count, channels, rows, _ = pattern_ref.shape
    upper = lax.broadcasted_iota(jnp.int32, (rows, LANES), 0) < rows // 2
    for n, ref in enumerate(blocks):
        for fb in range(count):
            block = ref[fb].astype(jnp.float32)
            for duo in range(channels // 2):
                tile = block[duo * rows : (duo + 1) * rows]
                turned = pltpu.roll(tile, rows // 2, 0)
                pattern_ref[n, fb, 2 * duo] = jnp.where(upper, tile, turned)
                pattern_ref[n, fb, 2 * duo + 1] = jnp.where(upper, turned, tile)


def tally(slots, far_ref, pattern_ref, cross_ref, pair_ref):
    _, blocks, channels, rows, _ = pattern_ref.shape
    half = blocks // 2
    duos = channels // 2
    for fb in range(half):
        for side in range(2):
            acc = {}
            for n, slot in enumerate(slots):
                far_re = far_ref[slot, side, fb].astype(jnp.float32)
                far_im = far_ref[slot, side, half + fb].astype(jnp.float32)
                for i in range(channels):
                    near_re = pattern_ref[n, fb, i]
                    near_im = pattern_ref[n, half + fb, i]
                    for duo in range(duos):
                        fr = far_re[duo * rows : (duo + 1) * rows]
                        fi = far_im[duo * rows : (duo + 1) * rows]
                        re = near_re * fr + near_im * fi
                        im = near_im * fr - near_re * fi
                        if n:
                            re = acc[i, duo][0] + re
                            im = acc[i, duo][1] + im
                        acc[i, duo] = (re, im)
            for (i, duo), value in acc.items():
                row = ((i * 2 + side) * duos + duo) * rows
                for part in range(2):
                    cross_ref[part, fb, row : row + rows] = value[part]
    for side in range(2):
        acc = {}
        for n, slot in enumerate(slots):
            far = far_ref[slot, side, 2 * half].astype(jnp.float32)
            for i in range(channels):
                near = pattern_ref[n, 2 * half, i]
                for duo in range(duos):
                    count = near * far[duo * rows : (duo + 1) * rows]
                    acc[i, duo] = acc[i, duo] + count if n else count
        for (i, duo), value in acc.items():
            row = ((i * 2 + side) * duos + duo) * rows
            pair_ref[row : row + rows] = value


def over_windows(ref, windows):
    lines = ref.shape[0] // windows
    return sum(ref[pl.ds(s, lines, stride=windows), :] for s in range(windows))


def near_slots(groups, core, own):
    pairs = [slots(blocks, core) for blocks in exchange_plan(groups)[groups // 2 : -1]]
    return [0, *(mine for mine, _ in pairs)] if own else [groups - 1, *(theirs for _, theirs in pairs)]


def gather_kernel(groups, *refs):
    refs = list(refs)
    take = lambda count: [refs.pop(0) for _ in range(count)]
    near_refs, direct_refs, passed_refs = take(groups // 2), take(groups // 2), take(groups // 2)
    far_ref, part_ref, count_ref, pattern_ref, cross_ref, pair_ref = refs
    windows = pattern_ref.shape[3] // 2
    core, turn = place(groups)
    for blocks, direct, passed in zip(exchange_plan(groups), direct_refs, passed_refs):
        mine, theirs = slots(blocks, core, turn)
        for side in range(2):
            far_ref[mine, side] = direct[side]
            far_ref[theirs, side] = passed[1 - side]
    spread([near_refs[0], *(ref.at[0] for ref in near_refs[1:])], pattern_ref)
    tally(near_slots(groups, core, True), far_ref, pattern_ref, cross_ref, pair_ref)
    for part in range(2):
        for fb in range(cross_ref.shape[1]):
            part_ref[part, fb] = over_windows(cross_ref.at[part, fb], windows)
    count_ref[...] = over_windows(pair_ref, windows)


def finish_kernel(groups, *refs):
    late_refs = refs[: groups // 2]
    far_ref, part_ref, count_ref, held_ref, out_ref, pattern_ref, cross_ref, pair_ref = refs[groups // 2 :]
    channels = pattern_ref.shape[2]
    windows = pattern_ref.shape[3] // 2
    core, _ = place(groups)
    spread(late_refs, pattern_ref)
    tally(near_slots(groups, core, False), far_ref, pattern_ref, cross_ref, pair_ref)

    def transform(part, p):
        span = range(p * BLOCK // LANES, (p + 1) * BLOCK // LANES)
        cross = [part_ref[part, fb] + over_windows(cross_ref.at[part, fb], windows) for fb in span]
        cross = jnp.concatenate(cross, axis=1)
        size = cross.shape[0]
        top = cross.astype(jnp.bfloat16)
        rest = (cross - top.astype(jnp.float32)).astype(jnp.bfloat16)
        both = jnp.dot(jnp.concatenate([top, rest], axis=0), held_ref[p, part], preferred_element_type=jnp.float32)
        return both[:size, :LANES] + (both[:size, LANES:] + both[size:, :LANES])

    cosine, sine = [sum(transform(part, p) for p in range(held_ref.shape[0])) for part in range(2)]
    pairs = jnp.maximum(count_ref[...] + over_windows(pair_ref, windows), 1.0)
    ahead = (cosine - sine) / pairs
    behind = (cosine + sine) / pairs
    lane = lax.broadcasted_iota(jnp.int32, behind.shape, 1)
    behind = jnp.take_along_axis(behind, jnp.maximum(MAXLAG - lane, 0), axis=1)
    ahead = pltpu.roll(ahead, MAXLAG, 1)
    result = jnp.concatenate([jnp.where(lane < MAXLAG, behind, ahead), ahead], axis=1)
    for i in range(channels):
        block = result[i * 2 * channels : (i + 1) * 2 * channels]
        block = jnp.where(core == 0, block, pltpu.roll(block, channels, 0))
        out_ref[i] = block[:, :NUM_LAGS]


def correlate(groups, near, far, late, table, channels, windows):
    count = near[0].shape[0]
    lines = channels * 2 * channels
    vmem = pl.BlockSpec(memory_space=pltpu.VMEM)
    hold = lambda values: [pltpu.with_memory_space_constraint(value, pltpu.VMEM) for value in values]
    scratch = [
        pltpu.VMEM((groups // 2, count, channels, 2 * windows, LANES), jnp.float32),
        pltpu.VMEM((2, count // 2, lines * windows, LANES), jnp.float32),
        pltpu.VMEM((lines * windows, LANES), jnp.float32),
    ]
    sums = pl.pallas_call(
        lambda *refs: gather_kernel(groups, *refs),
        out_shape=(
            pltpu.VMEM((groups, 2, *near[0].shape), near[0].dtype),
            pltpu.VMEM((2, count // 2, lines, LANES), jnp.float32),
            pltpu.VMEM((lines, LANES), jnp.float32),
        ),
        in_specs=[vmem] * (len(near) + len(far)),
        out_specs=(vmem, vmem, vmem),
        scratch_shapes=scratch,
        compiler_params=pltpu.CompilerParams(vmem_limit_bytes=VMEM_LIMIT),
        name="gather",
    )(*hold((*near, *far)))
    return pl.pallas_call(
        lambda *refs: finish_kernel(groups, *refs),
        out_shape=jax.ShapeDtypeStruct((channels, 2 * channels, NUM_LAGS), jnp.float32),
        in_specs=[vmem] * (len(late) + 4),
        out_specs=vmem,
        scratch_shapes=scratch,
        compiler_params=pltpu.CompilerParams(vmem_limit_bytes=VMEM_LIMIT),
        name="finish",
    )(*hold((*late, *sums, table)))


def solution(mesh):
    groups = mesh.shape["tm"]
    assert mesh.shape["chan"] == CORES * groups and groups & (groups - 1) == 0

    def route(move):
        pairs = []
        for line in range(groups):
            for core in range(CORES):
                for t in range(groups):
                    to_line, to_core, to_t = move(line, core, t)
                    source = (line * CORES + core) * groups + t
                    pairs.append((source, (to_line * CORES + to_core) * groups + to_t))
        return pairs

    def send(value, move):
        return lax.ppermute(value, ("chan", "tm"), route(move))

    def local(spectra, keep_mask):
        channels, windows, width = spectra.shape
        swap = lambda value: send(value, lambda line, core, t: (line, 1 - core, t))
        moves = {
            "far": lambda line, core, t, b: (t ^ b, core, line),
            "near": lambda line, core, t, k: (line, core, t ^ k),
        }

        def fetch(value, *blocks):
            def move(line, core, t):
                kind, number = blocks[core]
                return moves[kind](line, core, t, number)

            return send(value, move)

        kept = swap(keep_mask)
        sibling = swap(spectra), kept
        own, table = whiten(spectra, keep_mask, jnp.asarray(lag_table(width // 2)))
        chip = join(own, *sibling)
        plan = exchange_plan(groups)
        direct = [fetch(own if blocks[0] == blocks[1] else chip, *blocks) for blocks in plan]
        *direct, last = direct
        far, near = direct[: groups // 2], direct[groups // 2 :]
        far_passed = [swap(value) for value in far]
        late = [last, *(swap(value[1]) for value in near)]
        return correlate(groups, (own, *near), (*far, *far_passed), late, table, channels, windows)

    placed = (P("chan", "tm", None), P("chan", "tm"))
    return jax.shard_map(local, mesh=mesh, in_specs=placed, out_specs=P("chan", "tm", None), check_vma=False)
```
